32 devices in a mesh: groups: 2 (over x), rows: 2 (over core), cols: 8 (over z, y).
Axes of the slice: x: 2, y: 2, z: 4, core: 2. Of those that a mesh axis runs over, the one named last changes fastest.
Arguments:
- texture: float32 [8192, 8192], P(('groups', 'rows'), 'cols'), parts along dimension 0, as said below
- sketch: float32 [8192, 256], P('cols'), may hold values from -0.0625 to 0.0625
Outputs:
- projected: float32 [512, 8192], P(('groups', 'rows'), 'cols'), parts along dimension 0
The draws below stay inside these ranges and needn't reach their ends.
There are 2 independent parts, one for each index of `groups`. The reference program is written for one: setup_inputs(seed, part) draws one part's arguments, and reference() takes and returns one part's arrays. A program takes and returns all parts, laid end to end along the dimension named above; an argument that names none is the same for every part. Nothing has to cross between parts.
Inputs may be any that keep to these rules, and one draw needn't show every extreme that they name: `texture`: finite reals of moderate size.
All inputs are finite; a program needn't handle non-finite values.
Results may differ from the reference program's by a relative error of at most 0.00014.
Values sent between devices are 32-bit elements; how exact they have to be, the bound alone decides.
No kernel may reach another device: no remote copies, remote signals or barrier semaphores. Data moves between devices by JAX's collectives and lax.ppermute only.
A program may use at most 64 MiB of HBM per device.

```python
import math
import jax
import jax.numpy as jnp
from jax import lax

RANK = 256
TEXELS = 4096
SCANS = 8192


def draw_texture(key, part):
    key_row, key_col, key_base = jax.random.split(key, 3)
    position = jnp.arange(TEXELS, dtype=jnp.float32) / TEXELS
    row_scale = (1.0 + 2.0 * position) * jnp.exp(jax.random.uniform(key_row, (TEXELS,), jnp.float32, 0.0, math.log(4.0)))
    col_scale = jnp.exp(jax.random.uniform(key_col, (SCANS,), jnp.float32, 0.0, math.log(4.0)))
    base = jax.random.normal(key_base, (TEXELS, SCANS), jnp.float32)
    return 0.25 * base * row_scale[:, None] * col_scale[None, :]


def steps_of(own_key, extent, cuts, smallest, high):
    def one(dim, blocks):
        draws = jax.random.uniform(jax.random.fold_in(jax.random.fold_in(own_key, 6), dim), (blocks,), jnp.float32, smallest / len(cuts), high / len(cuts))
        return jnp.repeat(jnp.exp(draws), extent[dim] // blocks).reshape((-1,) + (1,) * (len(extent) - dim - 1))

    factor_of = one(*cuts[0])
    for cut in cuts[1:]:
        factor_of = factor_of * one(*cut)
    return factor_of


def gaussian(key, dims, scale, limit, cuts=(), kind=jnp.bfloat16):
    result = jax.random.normal(key, dims, jnp.float32) * scale
    if len(cuts) > 0:
        result = steps_of(key, dims, cuts, -0.22, 0.18) * result
    return jnp.clip(result, min=-limit, max=limit).astype(kind)


def setup_inputs(seed: int = 0, part: int = 0) -> dict:
    seeds = jax.random.split(jax.random.key(seed), 3)
    part_splits = jax.random.split(jax.random.fold_in(seeds[2], part), 3)
    texture = draw_texture(jax.random.fold_in(jax.random.fold_in(seeds[2], part), 71), part)
    sketch = gaussian(seeds[1], (SCANS, RANK), SCANS ** -0.5, 0.0625, ((0, 8),), jnp.float32)
    return dict(texture=texture, sketch=sketch)


def reference(texture, sketch):
    highest = lax.Precision.HIGHEST
    image = jnp.dot(texture.astype(jnp.float32), sketch.astype(jnp.float32), precision=highest, preferred_element_type=jnp.float32)
    gram = lax.dot_general(image.astype(jnp.float32), image.astype(jnp.float32), (((0,), (0,)), ((), ())), precision=highest, preferred_element_type=jnp.float32)
    lower = jnp.linalg.cholesky(gram)
    basis = lax.linalg.triangular_solve(lower, image, left_side=False, lower=True, transpose_a=True)
    projected = lax.dot_general(basis.astype(jnp.float32), texture.astype(jnp.float32), (((0,), (0,)), ((), ())), precision=highest, preferred_element_type=jnp.float32)
    return projected
```

```python
import jax
import jax.numpy as jnp
from jax import lax
from jax.sharding import PartitionSpec as P

HIGH = lax.Precision.HIGH
CHUNKS = 4


def inner_rows(left, right):
    return lax.dot_general(
        left,
        right,
        (((0,), (0,)), ((), ())),
        precision=HIGH,
        preferred_element_type=jnp.float32,
    )


def line_sum(part, place):
    inward = [(0 + y, 2 + y) for y in range(2)] + [(6 + y, 4 + y) for y in range(2)]
    across = [(2 + y, 4 + y) for y in range(2)] + [(4 + y, 2 + y) for y in range(2)]
    outward = [(2 + y, 0 + y) for y in range(2)] + [(4 + y, 6 + y) for y in range(2)]
    part = part + lax.ppermute(part, "cols", inward)
    part = part + lax.ppermute(part, "cols", across)
    far = lax.ppermute(part, "cols", outward)
    return jnp.where((place == 1) | (place == 2), part, far)


def per_device(texture, sketch):
    cols = lax.axis_size("cols")
    rows = texture.shape[0]
    gram = jnp.zeros((sketch.shape[1],) * 2, jnp.float32)
    product = jnp.zeros((sketch.shape[1], texture.shape[1]), jnp.float32)
    if cols == 8:
        col = lax.axis_index("cols")
        side, place = lax.rem(col, 2), lax.div(col, 2)
        swap = [(c, c ^ 1) for c in range(cols)]
        span = rows // (2 * CHUNKS)
        blocks, halves = [], []
        for chunk in range(CHUNKS):
            own = lax.dynamic_slice_in_dim(texture, (2 * chunk + side) * span, span)
            other = lax.dynamic_slice_in_dim(texture, (2 * chunk + 1 - side) * span, span)
            theirs = jnp.dot(other, sketch, precision=HIGH, preferred_element_type=jnp.float32)
            mine = jnp.dot(own, sketch, precision=HIGH, preferred_element_type=jnp.float32)
            mine = mine + lax.ppermute(theirs, "cols", swap)
            image = line_sum(mine, place)
            halves.append((own, image))
            halves.append((other, lax.ppermute(image, "cols", swap)))
        for block, image in halves:
            gram = gram + inner_rows(image, image)
            product = product + inner_rows(image, block)
    else:
        image = lax.psum(jnp.dot(texture, sketch, precision=HIGH, preferred_element_type=jnp.float32), "cols")
        gram = inner_rows(image, image)
        product = inner_rows(image, texture)
    pair = [(0, 1), (1, 0)]
    gram = gram + lax.ppermute(gram, "rows", pair)
    product = product + lax.ppermute(product, "rows", pair)
    lower = jnp.linalg.cholesky(gram)
    eye = jnp.eye(gram.shape[0], dtype=jnp.float32)
    inverse = lax.linalg.triangular_solve(lower, eye, left_side=True, lower=True)
    span = gram.shape[0] // lax.axis_size("rows")
    inverse = lax.dynamic_slice_in_dim(inverse, lax.axis_index("rows") * span, span)
    return jnp.dot(inverse, product, precision=HIGH, preferred_element_type=jnp.float32)


def solution(mesh):
    placed = (P(("groups", "rows"), "cols"), P("cols", None))
    return jax.shard_map(
        per_device,
        mesh=mesh,
        in_specs=placed,
        out_specs=P(("groups", "rows"), "cols"),
        check_vma=False,
    )
```

```python
import functools

import jax
import jax.numpy as jnp
from jax import lax
from jax.experimental import pallas as pl
from jax.experimental.pallas import tpu as pltpu
from jax.sharding import PartitionSpec as P

HIGH = lax.Precision.HIGH
SPANS = (160, 176, 176)
BLOCK = 64


def inner_rows(left, right):
    return lax.dot_general(
        left,
        right,
        (((0,), (0,)), ((), ())),
        precision=HIGH,
        preferred_element_type=jnp.float32,
    )


def small_dot(left, right, dims):
    return lax.dot_general(
        left,
        right,
        (dims, ((), ())),
        precision=lax.Precision.HIGHEST,
        preferred_element_type=jnp.float32,
    )


def inverse_factor(block):
    size = block.shape[0]
    row = lax.broadcasted_iota(jnp.int32, block.shape, 0)
    col = lax.broadcasted_iota(jnp.int32, block.shape, 1)
    rows = lax.broadcasted_iota(jnp.int32, (size, 1), 0)
    pivots = jnp.ones((size, 1), jnp.float32)
    for j in range(size):
        pivot = block[j : j + 1, j : j + 1]
        factor = jnp.where(rows > j, block[:, j : j + 1] * (1.0 / pivot), 0.0)
        pivots = jnp.where(rows == j, pivot, pivots)
        line = jnp.where(col[0:1] == j, 1.0, block[j : j + 1, :])
        block = jnp.where((col == j) & (row != j), 0.0, block) - factor * line
    unit = jnp.where(col == row, 1.0, jnp.where(col < row, block, 0.0))
    return unit * lax.rsqrt(pivots)


def factor_kernel(gram_ref, far_ref, out_ref, work):
    size = gram_ref.shape[0]
    work[...] = gram_ref[...] + far_ref[...]
    for start in range(0, size, BLOCK):
        stop = start + BLOCK
        corner = inverse_factor(work[start:stop, start:stop])
        lane = lax.broadcasted_iota(jnp.int32, (BLOCK, size), 1)
        wide = jnp.concatenate(
            [jnp.zeros((BLOCK, start), jnp.float32)] * (start > 0)
            + [corner]
            + [jnp.zeros((BLOCK, size - stop), jnp.float32)] * (stop < size),
            axis=1,
        )
        lines = small_dot(corner, work[start:stop, :], ((1,), (0,)))
        lines = jnp.where((lane >= start) & (lane < stop), wide, lines)
        out_ref[start:stop, :] = jnp.where(lane < stop, lines, 0.0)
        if stop < size:
            factor = small_dot(work[stop:, start:stop], corner, ((1,), (1,)))
            lane = lax.broadcasted_iota(jnp.int32, (size - stop, size), 1)
            old = jnp.where((lane >= start) & (lane < stop), 0.0, work[stop:, :])
            work[stop:, :] = old - small_dot(factor, lines, ((1,), (0,)))


def inverse_cholesky(gram, far):
    whole = pl.BlockSpec(memory_space=pltpu.VMEM)
    return pl.pallas_call(
        factor_kernel,
        out_shape=jax.ShapeDtypeStruct(gram.shape, jnp.float32),
        in_specs=[whole, whole],
        out_specs=whole,
        scratch_shapes=[pltpu.VMEM(gram.shape, jnp.float32)],
        cost_estimate=pl.CostEstimate(flops=40_000_000, bytes_accessed=12 * gram.size, transcendentals=0),
    )(gram, far)


def after(values, *earlier):
    out = lax.optimization_barrier(tuple(values) + earlier)
    return out[: len(values)]


def summed_halves(texture, sketch):
    col = lax.axis_index("cols")
    side, place = lax.rem(col, 2), lax.div(col, 2)
    odd = lax.rem(place, 2)
    swap = {step: [(c, c ^ step) for c in range(8)] for step in (1, 2, 4)}
    send = lambda x, step: lax.ppermute(x, "cols", swap[step])
    starts = [4 * sum(SPANS[:k]) for k in range(len(SPANS))]
    half_rows = lambda k, s: lax.dynamic_slice_in_dim(texture, starts[k] + s * (2 * SPANS[k]), 2 * SPANS[k])
    own = [half_rows(k, side) for k in range(3)]
    other = [half_rows(k, 1 - side) for k in range(3)]
    sketched = lambda rows: jnp.dot(rows, sketch, precision=HIGH, preferred_element_type=jnp.float32)
    part = lambda x, k, which: lax.dynamic_slice_in_dim(x, which * SPANS[k], SPANS[k])

    def joined(mine, theirs):
        return jnp.where(odd == 0, jnp.concatenate([mine, theirs]), jnp.concatenate([theirs, mine]))

    y = [None] * 3
    quarter, other_quarter, half, far = [None] * 3, [None] * 3, [None] * 3, [None] * 3

    theirs = [sketched(x) for x in other]
    y[0] = send(theirs[0], 1)
    y[1] = send(theirs[1], 1)

    def settle(k):
        total = sketched(own[k]) + y[k]
        return part(total, k, odd), part(total, k, 1 - odd)

    quarter[0], out0 = settle(0)
    got0 = send(out0, 2)
    (theirs2,) = after([theirs[2]], y[0])
    y[2] = send(theirs2, 1)
    quarter[0] = quarter[0] + got0
    q0 = send(quarter[0], 4)
    quarter[1], out1 = settle(1)
    (out1,) = after([out1], got0)
    got1 = send(out1, 2)
    quarter[0] = quarter[0] + q0
    other_quarter[0] = send(quarter[0], 2)
    quarter[1] = quarter[1] + got1
    (s1,) = after([quarter[1]], q0)
    q1 = send(s1, 4)
    half[0] = joined(quarter[0], other_quarter[0])
    far[0] = send(half[0], 1)
    quarter[2], out2 = settle(2)
    (out2,) = after([out2], other_quarter[0])
    got2 = send(out2, 2)
    quarter[1] = quarter[1] + q1
    other_quarter[1] = send(quarter[1], 2)
    quarter[2] = quarter[2] + got2
    (s2,) = after([quarter[2]], q1)
    q2 = send(s2, 4)
    half[1] = joined(quarter[1], other_quarter[1])
    far[1] = send(half[1], 1)
    quarter[2] = quarter[2] + q2
    other_quarter[2] = send(quarter[2], 2)
    half[2] = joined(quarter[2], other_quarter[2])
    far[2] = send(half[2], 1)
    pairs = []
    for k in range(3):
        pairs += [(own[k], half[k]), (other[k], far[k])]
    return pairs


def per_device(texture, sketch):
    if lax.axis_size("cols") == 8 and texture.shape[0] == 4 * sum(SPANS):
        pairs = summed_halves(texture, sketch)
    else:
        partial = jnp.dot(texture, sketch, precision=HIGH, preferred_element_type=jnp.float32)
        pairs = [(texture, lax.psum(partial, "cols"))]
    gram, product = 0.0, 0.0
    for rows, image in pairs:
        gram = gram + inner_rows(image, image)
        product = product + inner_rows(image, rows)
    pair = [(0, 1), (1, 0)]
    inverse = inverse_cholesky(gram, lax.ppermute(gram, "rows", pair))
    product = product + lax.ppermute(product, "rows", pair)
    span = gram.shape[0] // lax.axis_size("rows")
    inverse = lax.dynamic_slice_in_dim(inverse, lax.axis_index("rows") * span, span)
    return jnp.dot(inverse, product, precision=HIGH, preferred_element_type=jnp.float32)


def solution(mesh):
    placed = (P(("groups", "rows"), "cols"), P("cols", None))
    return jax.shard_map(
        per_device,
        mesh=mesh,
        in_specs=placed,
        out_specs=P(("groups", "rows"), "cols"),
        check_vma=False,
    )
```

```python
import functools

import jax
import jax.numpy as jnp
from jax import lax
from jax.experimental import pallas as pl
from jax.experimental.pallas import tpu as pltpu
from jax.sharding import PartitionSpec as P

HIGH = lax.Precision.HIGH
ROWS = 128
WIDTH = 256
BLOCK = 64
LIGHT = pl.CostEstimate(flops=1000, bytes_accessed=1000, transcendentals=0)


def split(x):
    high = x.astype(jnp.bfloat16)
    return high, (x - high.astype(jnp.float32)).astype(jnp.bfloat16)


def three_passes(left, right, dims):
    (left_high, left_low), (right_high, right_low) = left, right
    dot = lambda x, y: lax.dot_general(x, y, (dims, ((), ())), preferred_element_type=jnp.float32)
    return dot(left_high, right_high) + (dot(left_low, right_high) + dot(left_high, right_low))


def sketch_kernel(blocks_ref, texture_ref, sketch_ref, *rest):
    outs, (high, low) = rest[:-2], rest[-2:]
    step = pl.program_id(0)

    @pl.when(step == 0)
    def _():
        high[...], low[...] = split(sketch_ref[...])

    result = three_passes(split(texture_ref[...]), (high[...], low[...]), ((1,), (0,)))
    for k, out in enumerate(outs):
        for part in range(2):

            @pl.when(step == 2 * k + part)
            def _():
                out[part * ROWS : (part + 1) * ROWS, :] = result


def sketched(texture, sketch, halves, earlier=()):
    blocks = jnp.stack([2 * h + part for h in halves for part in range(2)]).astype(jnp.int32)
    if earlier:
        (blocks,) = after([blocks], *earlier)
    scans, rank = sketch.shape
    whole = pl.BlockSpec(memory_space=pltpu.VMEM)
    work = 2 * len(halves) * ROWS
    return pl.pallas_call(
        sketch_kernel,
        out_shape=[jax.ShapeDtypeStruct((2 * ROWS, rank), jnp.float32)] * len(halves),
        grid_spec=pltpu.PrefetchScalarGridSpec(
            num_scalar_prefetch=1,
            grid=(2 * len(halves),),
            in_specs=[pl.BlockSpec((ROWS, scans), lambda i, b: (b[i], 0)), whole],
            out_specs=[whole] * len(halves),
            scratch_shapes=[pltpu.VMEM((scans, rank), jnp.bfloat16)] * 2,
        ),
        compiler_params=pltpu.CompilerParams(vmem_limit_bytes=16 << 20),
        cost_estimate=LIGHT,
    )(blocks, texture, sketch)


def gather_kernel(block_ref, image_ref, texture_ref, *rest):
    if len(rest) == 2:
        gram_ref, product_ref = rest
        old_gram = old_product = None
    else:
        old_gram, old_product, gram_ref, product_ref = rest
    image = split(image_ref[...].T)

    @pl.when(pl.program_id(0) == 0)
    def _():
        rows = split(image_ref[...])
        term = three_passes(image, rows, ((1,), (0,)))
        gram_ref[...] = term if old_gram is None else old_gram[...] + term

    term = three_passes(image, split(texture_ref[...]), ((1,), (0,)))
    product_ref[...] = term if old_product is None else old_product[...] + term


def gathered(half, image, texture, sums):
    rank, scans = image.shape[1], texture.shape[1]
    whole = pl.BlockSpec((rank, rank), lambda i, b: (0, 0))
    line = pl.BlockSpec((rank, WIDTH), lambda i, b: (0, i))
    return pl.pallas_call(
        gather_kernel,
        out_shape=[jax.ShapeDtypeStruct((rank, rank), jnp.float32), jax.ShapeDtypeStruct((rank, scans), jnp.float32)],
        grid_spec=pltpu.PrefetchScalarGridSpec(
            num_scalar_prefetch=1,
            grid=(scans // WIDTH,),
            in_specs=[
                pl.BlockSpec((2 * ROWS, rank), lambda i, b: (0, 0)),
                pl.BlockSpec((2 * ROWS, WIDTH), lambda i, b: (b[0], i)),
            ]
            + [whole, line][: len(sums)],
            out_specs=[whole, line],
        ),
        input_output_aliases={3: 0, 4: 1} if sums else {},
        compiler_params=pltpu.CompilerParams(vmem_limit_bytes=16 << 20),
        cost_estimate=LIGHT,
    )(half.reshape(1), image, texture, *sums)


def inner_rows(left, right):
    return lax.dot_general(
        left,
        right,
        (((0,), (0,)), ((), ())),
        precision=HIGH,
        preferred_element_type=jnp.float32,
    )


def small_dot(left, right, dims):
    return lax.dot_general(
        left,
        right,
        (dims, ((), ())),
        precision=lax.Precision.HIGHEST,
        preferred_element_type=jnp.float32,
    )


def inverse_factor(block):
    size = block.shape[0]
    row = lax.broadcasted_iota(jnp.int32, block.shape, 0)
    col = lax.broadcasted_iota(jnp.int32, block.shape, 1)
    rows = lax.broadcasted_iota(jnp.int32, (size, 1), 0)
    pivots = jnp.ones((size, 1), jnp.float32)
    for j in range(size):
        pivot = block[j : j + 1, j : j + 1]
        factor = jnp.where(rows > j, block[:, j : j + 1] * (1.0 / pivot), 0.0)
        pivots = jnp.where(rows == j, pivot, pivots)
        line = jnp.where(col[0:1] == j, 1.0, block[j : j + 1, :])
        block = jnp.where((col == j) & (row != j), 0.0, block) - factor * line
    unit = jnp.where(col == row, 1.0, jnp.where(col < row, block, 0.0))
    return unit * lax.rsqrt(pivots)


def factor_kernel(gram_ref, far_ref, out_ref, work):
    size = gram_ref.shape[0]
    work[...] = gram_ref[...] + far_ref[...]
    for start in range(0, size, BLOCK):
        stop = start + BLOCK
        corner = inverse_factor(work[start:stop, start:stop])
        lane = lax.broadcasted_iota(jnp.int32, (BLOCK, size), 1)
        wide = jnp.concatenate(
            [jnp.zeros((BLOCK, start), jnp.float32)] * (start > 0)
            + [corner]
            + [jnp.zeros((BLOCK, size - stop), jnp.float32)] * (stop < size),
            axis=1,
        )
        lines = small_dot(corner, work[start:stop, :], ((1,), (0,)))
        lines = jnp.where((lane >= start) & (lane < stop), wide, lines)
        out_ref[start:stop, :] = jnp.where(lane < stop, lines, 0.0)
        if stop < size:
            factor = small_dot(work[stop:, start:stop], corner, ((1,), (1,)))
            lane = lax.broadcasted_iota(jnp.int32, (size - stop, size), 1)
            old = jnp.where((lane >= start) & (lane < stop), 0.0, work[stop:, :])
            work[stop:, :] = old - small_dot(factor, lines, ((1,), (0,)))


def inverse_cholesky(gram, far):
    whole = pl.BlockSpec(memory_space=pltpu.VMEM)
    return pl.pallas_call(
        factor_kernel,
        out_shape=jax.ShapeDtypeStruct(gram.shape, jnp.float32),
        in_specs=[whole, whole],
        out_specs=whole,
        scratch_shapes=[pltpu.VMEM(gram.shape, jnp.float32)],
        compiler_params=pltpu.CompilerParams(vmem_limit_bytes=16 << 20),
        cost_estimate=LIGHT,
    )(gram, far)


def after(values, *earlier):
    out = lax.optimization_barrier(tuple(values) + earlier)
    return out[: len(values)]


def exchanged(texture, sketch):
    col = lax.axis_index("cols")
    side, place = lax.rem(col, 2), lax.div(col, 2)
    odd = lax.rem(place, 2)
    pairs = {step: [(c, c ^ step) for c in range(8)] for step in (1, 2, 4)}
    chunks = range(texture.shape[0] // (4 * ROWS))
    mine = [2 * k + side for k in chunks]
    theirs = [2 * k + 1 - side for k in chunks]
    last = [None]
    texture = pltpu.with_memory_space_constraint(texture, pltpu.HBM)

    def send(x, step):
        last[0] = x
        return lax.ppermute(x, "cols", pairs[step])

    def part(x, which):
        return lax.dynamic_slice_in_dim(x, which * ROWS, ROWS)

    def joined(own, other):
        return jnp.where(odd == 0, jnp.concatenate([own, other]), jnp.concatenate([other, own]))

    outward = []
    for h in theirs:
        outward += sketched(texture, sketch, [h], outward[-1:])
    y = [send(x, 1) for x in outward]
    own = sketched(texture, sketch, mine, outward[-1:])
    kept, half, far, sums = {}, {}, {}, [()]
    arriving = dict(enumerate(y))

    def arrived(k):
        (x,) = after([arriving[k]], last[0])
        return x

    def to_pair(k):
        total = own[k] + arrived(k)
        kept[k] = part(total, odd)
        arriving[k] = send(part(total, 1 - odd), 2)

    def to_line(k):
        kept[k] = kept[k] + arrived(k)
        arriving[k] = send(kept[k], 4)

    def back_to_pair(k):
        kept[k] = kept[k] + arrived(k)
        arriving[k] = send(kept[k], 2)

    def back_to_side(k):
        half[k] = joined(kept[k], arrived(k))
        arriving[k] = send(half[k], 1)

    def gather_own(k):
        (image,) = after([half[k]], last[0])
        sums[0] = gathered(mine[k], image, texture, sums[0])
        last[0] = sums[0][0]

    def gather_far(k):
        sums[0] = gathered(theirs[k], arrived(k), texture, sums[0])
        last[0] = sums[0][0]

    to_p, to_l, to_b, to_s, own_g, far_g = to_pair, to_line, back_to_pair, back_to_side, gather_own, gather_far
    order = [(to_p, 0), (to_p, 1), (to_l, 0), (to_p, 2), (to_l, 1), (to_b, 0), (to_p, 3), (to_l, 2), (to_s, 0)]
    order += [(to_b, 1), (to_l, 3), (own_g, 0), (to_s, 1), (to_b, 2), (own_g, 1), (far_g, 0), (to_b, 3), (to_s, 2)]
    order += [(own_g, 2), (far_g, 1), (to_s, 3), (own_g, 3), (far_g, 2), (far_g, 3)]
    for step, k in order:
        step(k)
    sums = sums[0]
    return sums


def per_device(texture, sketch):
    if lax.axis_size("cols") == 8 and texture.shape[0] == 16 * ROWS:
        gram, product = exchanged(texture, sketch)
    else:
        partial = jnp.dot(texture, sketch, precision=HIGH, preferred_element_type=jnp.float32)
        image = lax.psum(partial, "cols")
        gram, product = inner_rows(image, image), inner_rows(image, texture)
    pair = [(0, 1), (1, 0)]
    far = lax.ppermute(gram, "rows", pair)
    inverse = inverse_cholesky(gram, far)
    (product,) = after([product], far)
    product = product + lax.ppermute(product, "rows", pair)
    span = gram.shape[0] // lax.axis_size("rows")
    inverse = lax.dynamic_slice_in_dim(inverse, lax.axis_index("rows") * span, span)
    return jnp.dot(inverse, product, precision=HIGH, preferred_element_type=jnp.float32)


def solution(mesh):
    placed = (P(("groups", "rows"), "cols"), P("cols", None))
    return jax.shard_map(
        per_device,
        mesh=mesh,
        in_specs=placed,
        out_specs=P(("groups", "rows"), "cols"),
        check_vma=False,
    )
```

```python
import functools

import jax
import jax.numpy as jnp
from jax import lax
from jax.experimental import pallas as pl
from jax.experimental.pallas import tpu as pltpu
from jax.sharding import PartitionSpec as P

HIGH = lax.Precision.HIGH
ROWS = 128
BLOCK = 64
LIGHT = pl.CostEstimate(flops=1000, bytes_accessed=1000, transcendentals=0)


def inner_rows(left, right):
    return lax.dot_general(
        left,
        right,
        (((0,), (0,)), ((), ())),
        precision=HIGH,
        preferred_element_type=jnp.float32,
    )


def small_dot(left, right, dims):
    return lax.dot_general(
        left,
        right,
        (dims, ((), ())),
        precision=lax.Precision.HIGHEST,
        preferred_element_type=jnp.float32,
    )


def inverse_factor(block):
    size = block.shape[0]
    row = lax.broadcasted_iota(jnp.int32, block.shape, 0)
    col = lax.broadcasted_iota(jnp.int32, block.shape, 1)
    rows = lax.broadcasted_iota(jnp.int32, (size, 1), 0)
    pivots = jnp.ones((size, 1), jnp.float32)
    for j in range(size):
        pivot = block[j : j + 1, j : j + 1]
        factor = jnp.where(rows > j, block[:, j : j + 1] * (1.0 / pivot), 0.0)
        pivots = jnp.where(rows == j, pivot, pivots)
        line = jnp.where(col[0:1] == j, 1.0, block[j : j + 1, :])
        block = jnp.where((col == j) & (row != j), 0.0, block) - factor * line
    unit = jnp.where(col == row, 1.0, jnp.where(col < row, block, 0.0))
    return unit * lax.rsqrt(pivots)


def factor_kernel(gram_ref, far_ref, out_ref, work):
    size = gram_ref.shape[0]
    work[...] = gram_ref[...] + far_ref[...]
    for start in range(0, size, BLOCK):
        stop = start + BLOCK
        corner = inverse_factor(work[start:stop, start:stop])
        lane = lax.broadcasted_iota(jnp.int32, (BLOCK, size), 1)
        wide = jnp.concatenate(
            [jnp.zeros((BLOCK, start), jnp.float32)] * (start > 0)
            + [corner]
            + [jnp.zeros((BLOCK, size - stop), jnp.float32)] * (stop < size),
            axis=1,
        )
        lines = small_dot(corner, work[start:stop, :], ((1,), (0,)))
        lines = jnp.where((lane >= start) & (lane < stop), wide, lines)
        out_ref[start:stop, :] = jnp.where(lane < stop, lines, 0.0)
        if stop < size:
            factor = small_dot(work[stop:, start:stop], corner, ((1,), (1,)))
            lane = lax.broadcasted_iota(jnp.int32, (size - stop, size), 1)
            old = jnp.where((lane >= start) & (lane < stop), 0.0, work[stop:, :])
            work[stop:, :] = old - small_dot(factor, lines, ((1,), (0,)))


def inverse_cholesky(gram, far):
    whole = pl.BlockSpec(memory_space=pltpu.VMEM)
    return pl.pallas_call(
        factor_kernel,
        out_shape=jax.ShapeDtypeStruct(gram.shape, jnp.float32),
        in_specs=[whole, whole],
        out_specs=whole,
        scratch_shapes=[pltpu.VMEM(gram.shape, jnp.float32)],
        compiler_params=pltpu.CompilerParams(vmem_limit_bytes=16 << 20),
        cost_estimate=LIGHT,
    )(gram, far)


def after(values, *earlier):
    out = lax.optimization_barrier(tuple(values) + earlier)
    return out[: len(values)]


def exchanged(texture, sketch):
    col = lax.axis_index("cols")
    side, place = lax.rem(col, 2), lax.div(col, 2)
    odd = lax.rem(place, 2)
    pairs = {step: [(c, c ^ step) for c in range(8)] for step in (1, 2, 4)}
    chunks = range(texture.shape[0] // (4 * ROWS))
    mine = [2 * k + side for k in chunks]
    theirs = [2 * k + 1 - side for k in chunks]
    last = [None]

    def send(x, step):
        last[0] = x
        return lax.ppermute(x, "cols", pairs[step])

    def rows_of(h):
        return lax.dynamic_slice_in_dim(texture, 2 * ROWS * h, 2 * ROWS)

    def sketched(h, *earlier):
        (weights,) = after([sketch], *earlier)
        return jnp.dot(rows_of(h), weights, precision=HIGH, preferred_element_type=jnp.float32)

    def part(x, which):
        return lax.dynamic_slice_in_dim(x, which * ROWS, ROWS)

    def joined(own, other):
        return jnp.where(odd == 0, jnp.concatenate([own, other]), jnp.concatenate([other, own]))

    outward, own = [], []
    for h in theirs:
        outward.append(sketched(h, *outward[-1:]))
    y = [send(x, 1) for x in outward]
    for h in mine:
        own.append(sketched(h, (own or outward)[-1]))
    kept, half, far, sums = {}, {}, {}, [()]
    arriving = dict(enumerate(y))

    def arrived(k):
        (x,) = after([arriving[k]], last[0])
        return x

    def to_pair(k):
        total = own[k] + arrived(k)
        kept[k] = part(total, odd)
        arriving[k] = send(part(total, 1 - odd), 2)

    def to_line(k):
        kept[k] = kept[k] + arrived(k)
        arriving[k] = send(kept[k], 4)

    def back_to_pair(k):
        kept[k] = kept[k] + arrived(k)
        arriving[k] = send(kept[k], 2)

    def back_to_side(k):
        half[k] = joined(kept[k], arrived(k))
        arriving[k] = send(half[k], 1)

    def gather(rows, image):
        terms = inner_rows(image, image), inner_rows(image, rows)
        sums[0] = lax.optimization_barrier(tuple(map(jnp.add, sums[0], terms)) if sums[0] else terms)
        last[0] = sums[0][0]

    def gather_own(k):
        gather(rows_of(mine[k]), *after([half[k]], last[0]))

    def gather_far(k):
        gather(rows_of(theirs[k]), arrived(k))

    to_p, to_l, to_b, to_s, own_g, far_g = to_pair, to_line, back_to_pair, back_to_side, gather_own, gather_far
    order = [(to_p, 0), (to_p, 1), (to_l, 0), (to_p, 2), (to_l, 1), (to_b, 0), (to_p, 3), (to_l, 2), (to_s, 0)]
    order += [(to_b, 1), (to_l, 3), (own_g, 0), (to_s, 1), (to_b, 2), (own_g, 1), (to_b, 3), (far_g, 0), (to_s, 2)]
    order += [(own_g, 2), (far_g, 1), (to_s, 3), (own_g, 3), (far_g, 2), (far_g, 3)]
    for step, k in order:
        step(k)
    sums = sums[0]
    return sums


def per_device(texture, sketch):
    if lax.axis_size("cols") == 8 and texture.shape[0] == 16 * ROWS:
        gram, product = exchanged(texture, sketch)
    else:
        partial = jnp.dot(texture, sketch, precision=HIGH, preferred_element_type=jnp.float32)
        image = lax.psum(partial, "cols")
        gram, product = inner_rows(image, image), inner_rows(image, texture)
    pair = [(0, 1), (1, 0)]
    far = lax.ppermute(gram, "rows", pair)
    inverse = inverse_cholesky(gram, far)
    (product,) = after([product], far)
    product = product + lax.ppermute(product, "rows", pair)
    span = gram.shape[0] // lax.axis_size("rows")
    inverse = lax.dynamic_slice_in_dim(inverse, lax.axis_index("rows") * span, span)
    return jnp.dot(inverse, product, precision=HIGH, preferred_element_type=jnp.float32)


def solution(mesh):
    placed = (P(("groups", "rows"), "cols"), P("cols", None))
    return jax.shard_map(
        per_device,
        mesh=mesh,
        in_specs=placed,
        out_specs=P(("groups", "rows"), "cols"),
        check_vma=False,
    )
```

```python
import functools

import jax
import jax.numpy as jnp
from jax import lax
from jax.experimental import pallas as pl
from jax.experimental.pallas import tpu as pltpu
from jax.sharding import PartitionSpec as P

HIGH = lax.Precision.HIGH
SIZES = (128, 256, 128)
MATMULS = [(0, True), (1, True), (0, False), (2, True), (1, False), (2, False)]
STEPS = [("i", 0), ("l", 0), ("i", 1), ("i", 2), ("b", 0), ("l", 1), ("l", 2), ("o", 0), ("b", 1), ("g", 0), ("f", 0)]
STEPS += [("o", 1), ("b", 2), ("g", 1), ("o", 2), ("f", 1), ("g", 2), ("f", 2)]
BLOCK = 64
LIGHT = pl.CostEstimate(flops=1000, bytes_accessed=1000, transcendentals=0)


def inner_rows(left, right):
    return lax.dot_general(
        left,
        right,
        (((0,), (0,)), ((), ())),
        precision=HIGH,
        preferred_element_type=jnp.float32,
    )


def small_dot(left, right, dims):
    return lax.dot_general(
        left,
        right,
        (dims, ((), ())),
        precision=lax.Precision.HIGHEST,
        preferred_element_type=jnp.float32,
    )


def inverse_factor(block):
    size = block.shape[0]
    row = lax.broadcasted_iota(jnp.int32, block.shape, 0)
    col = lax.broadcasted_iota(jnp.int32, block.shape, 1)
    rows = lax.broadcasted_iota(jnp.int32, (size, 1), 0)
    pivots = jnp.ones((size, 1), jnp.float32)
    for j in range(size):
        pivot = block[j : j + 1, j : j + 1]
        factor = jnp.where(rows > j, block[:, j : j + 1] * (1.0 / pivot), 0.0)
        pivots = jnp.where(rows == j, pivot, pivots)
        line = jnp.where(col[0:1] == j, 1.0, block[j : j + 1, :])
        block = jnp.where((col == j) & (row != j), 0.0, block) - factor * line
    unit = jnp.where(col == row, 1.0, jnp.where(col < row, block, 0.0))
    return unit * lax.rsqrt(pivots)


def factor_kernel(gram_ref, far_ref, out_ref, work):
    size = gram_ref.shape[0]
    work[...] = gram_ref[...] + far_ref[...]
    for start in range(0, size, BLOCK):
        stop = start + BLOCK
        corner = inverse_factor(work[start:stop, start:stop])
        lane = lax.broadcasted_iota(jnp.int32, (BLOCK, size), 1)
        wide = jnp.concatenate(
            [jnp.zeros((BLOCK, start), jnp.float32)] * (start > 0)
            + [corner]
            + [jnp.zeros((BLOCK, size - stop), jnp.float32)] * (stop < size),
            axis=1,
        )
        lines = small_dot(corner, work[start:stop, :], ((1,), (0,)))
        lines = jnp.where((lane >= start) & (lane < stop), wide, lines)
        out_ref[start:stop, :] = jnp.where(lane < stop, lines, 0.0)
        if stop < size:
            factor = small_dot(work[stop:, start:stop], corner, ((1,), (1,)))
            lane = lax.broadcasted_iota(jnp.int32, (size - stop, size), 1)
            old = jnp.where((lane >= start) & (lane < stop), 0.0, work[stop:, :])
            work[stop:, :] = old - small_dot(factor, lines, ((1,), (0,)))


def inverse_cholesky(gram, far):
    whole = pl.BlockSpec(memory_space=pltpu.VMEM)
    return pl.pallas_call(
        factor_kernel,
        out_shape=jax.ShapeDtypeStruct(gram.shape, jnp.float32),
        in_specs=[whole, whole],
        out_specs=whole,
        scratch_shapes=[pltpu.VMEM(gram.shape, jnp.float32)],
        compiler_params=pltpu.CompilerParams(vmem_limit_bytes=16 << 20),
        cost_estimate=LIGHT,
    )(gram, far)


def after(values, *earlier):
    out = lax.optimization_barrier(tuple(values) + earlier)
    return out[: len(values)]


def exchanged(texture, sketch):
    col, row = lax.axis_index("cols"), lax.axis_index("rows")
    bits = lax.rem(col, 2), lax.rem(lax.div(col, 2), 2)
    side = jnp.where(row == 0, bits[0], bits[1])
    odd = jnp.where(row == 0, bits[1], bits[0])

    def pairs(first_core, second_core):
        return [(8 * r + c, 8 * r + (c ^ step)) for r, step in ((0, first_core), (1, second_core)) for c in range(8)]

    outer, inner, line = pairs(1, 2), pairs(2, 1), pairs(4, 4)
    chunks = range(len(SIZES))
    starts = [4 * sum(SIZES[:k]) for k in chunks]
    last = [None]

    def send(x, targets):
        last[0] = x
        return lax.ppermute(x, ("rows", "cols"), targets)

    def rows_of(k, which):
        return lax.dynamic_slice_in_dim(texture, starts[k] + which * (2 * SIZES[k]), 2 * SIZES[k])

    def sketched(k, which, *earlier):
        (weights,) = after([sketch], *earlier)
        return jnp.dot(rows_of(k, which), weights, precision=HIGH, preferred_element_type=jnp.float32)

    def part(x, which):
        return lax.dynamic_slice_in_dim(x, which * (x.shape[0] // 2), x.shape[0] // 2)

    def joined(own, other):
        return jnp.where(odd == 0, jnp.concatenate([own, other]), jnp.concatenate([other, own]))

    arriving, own, made = {}, {}, ()
    for k, theirs in MATMULS:
        made = (sketched(k, 1 - side if theirs else side, *made),)
        if theirs:
            arriving[k] = send(made[0], outer)
        else:
            own[k] = made[0]
    kept, half, sums = {}, {}, [()]

    def arrived(k):
        return after([arriving[k]], last[0])[0]

    def to_inner(k):
        total = own[k] + arrived(k)
        kept[k] = part(total, odd)
        arriving[k] = send(part(total, 1 - odd), inner)

    def to_line(k):
        kept[k] = kept[k] + arrived(k)
        arriving[k] = send(kept[k], line)

    def back_to_inner(k):
        kept[k] = kept[k] + arrived(k)
        arriving[k] = send(kept[k], inner)

    def back_to_outer(k):
        half[k] = joined(kept[k], arrived(k))
        arriving[k] = send(half[k], outer)

    def gather(rows, image):
        terms = inner_rows(image, image), inner_rows(image, rows)
        sums[0] = lax.optimization_barrier(tuple(map(jnp.add, sums[0], terms)) if sums[0] else terms)
        last[0] = sums[0][0]

    def gather_own(k):
        gather(rows_of(k, side), *after([half[k]], last[0]))

    def gather_far(k):
        gather(rows_of(k, 1 - side), arrived(k))

    steps = dict(i=to_inner, l=to_line, b=back_to_inner, o=back_to_outer, g=gather_own, f=gather_far)
    for name, k in STEPS:
        steps[name](k)
    return sums[0]


def per_device(texture, sketch):
    if lax.axis_size("cols") == 8 and texture.shape[0] == 4 * sum(SIZES):
        gram, product = exchanged(texture, sketch)
    else:
        partial = jnp.dot(texture, sketch, precision=HIGH, preferred_element_type=jnp.float32)
        image = lax.psum(partial, "cols")
        gram, product = inner_rows(image, image), inner_rows(image, texture)
    pair = [(0, 1), (1, 0)]
    far = lax.ppermute(gram, "rows", pair)
    inverse = inverse_cholesky(gram, far)
    (product,) = after([product], far)
    product = product + lax.ppermute(product, "rows", pair)
    span = gram.shape[0] // lax.axis_size("rows")
    inverse = lax.dynamic_slice_in_dim(inverse, lax.axis_index("rows") * span, span)
    return jnp.dot(inverse, product, precision=HIGH, preferred_element_type=jnp.float32)


def solution(mesh):
    placed = (P(("groups", "rows"), "cols"), P("cols", None))
    return jax.shard_map(
        per_device,
        mesh=mesh,
        in_specs=placed,
        out_specs=P(("groups", "rows"), "cols"),
        check_vma=False,
    )
```

```python
import functools

import jax
import jax.numpy as jnp
from jax import lax
from jax.experimental import pallas as pl
from jax.experimental.pallas import tpu as pltpu
from jax.sharding import PartitionSpec as P

HIGH = lax.Precision.HIGH
STEP = 256
SIZES = (128, 256, 128)
STEPS = [("m", [(0, True)]), ("m", [(1, True), (0, False)]), ("i", 0), ("m", [(2, True), (1, False), (2, False)])]
STEPS += [("l", 0), ("i", 1), ("b", 0), ("i", 2), ("l", 1), ("l", 2), ("o", 0), ("g", 0), ("f", 0), ("b", 1)]
STEPS += [("o", 1), ("b", 2), ("g", 1), ("o", 2), ("f", 1), ("g", 2), ("f", 2)]
BLOCK = 64
LIGHT = pl.CostEstimate(flops=1000, bytes_accessed=1000, transcendentals=0)


def split(x):
    high = x.astype(jnp.bfloat16)
    return high, (x - high.astype(jnp.float32)).astype(jnp.bfloat16)


def three_passes(left, right):
    (left_high, left_low), (right_high, right_low) = left, right
    dot = lambda x, y: jnp.dot(x, y, preferred_element_type=jnp.float32)
    return dot(left_high, right_high) + (dot(left_low, right_high) + dot(left_high, right_low))


def sketch_kernel(starts_ref, texture_ref, sketch_ref, *rest):
    outs, (blocks, sketch, sems) = rest[:-3], rest[-3:]
    count = blocks.shape[0]
    fetch = [pltpu.make_async_copy(sketch_ref, sketch, sems.at[count])]
    for k in range(count):
        start = pl.multiple_of(starts_ref[k], STEP)
        fetch.append(pltpu.make_async_copy(texture_ref.at[pl.ds(start, STEP), :], blocks.at[k], sems.at[k]))
    for copy in fetch:
        copy.start()
    fetch[0].wait()
    weights = split(sketch[...])
    k = 0
    for out in outs:
        for row in range(0, out.shape[0], STEP):
            fetch[k + 1].wait()
            out[row : row + STEP, :] = three_passes(split(blocks[k]), weights)
            k += 1


def sketched(texture, sketch, parts, earlier):
    starts = [first + row for first, length in parts for row in range(0, length, STEP)]
    (starts,) = after([jnp.stack(starts).astype(jnp.int32)], *earlier)
    count, (scans, rank) = starts.shape[0], sketch.shape
    there = pl.BlockSpec(memory_space=pl.ANY)
    return pl.pallas_call(
        sketch_kernel,
        out_shape=[jax.ShapeDtypeStruct((length, rank), jnp.float32) for _, length in parts],
        in_specs=[pl.BlockSpec(memory_space=pltpu.SMEM), there, there],
        out_specs=[pl.BlockSpec(memory_space=pltpu.VMEM)] * len(parts),
        scratch_shapes=[
            pltpu.VMEM((count, STEP, scans), jnp.float32),
            pltpu.VMEM((scans, rank), jnp.float32),
            pltpu.SemaphoreType.DMA((count + 1,)),
        ],
        compiler_params=pltpu.CompilerParams(vmem_limit_bytes=16 << 20),
        cost_estimate=pl.CostEstimate(
            flops=6 * count * STEP * scans * rank, bytes_accessed=4 * scans * (count * STEP + rank), transcendentals=0
        ),
    )(starts, texture, sketch)


def inner_rows(left, right):
    return lax.dot_general(
        left,
        right,
        (((0,), (0,)), ((), ())),
        precision=HIGH,
        preferred_element_type=jnp.float32,
    )


def small_dot(left, right, dims):
    return lax.dot_general(
        left,
        right,
        (dims, ((), ())),
        precision=lax.Precision.HIGHEST,
        preferred_element_type=jnp.float32,
    )


def inverse_factor(block):
    size = block.shape[0]
    row = lax.broadcasted_iota(jnp.int32, block.shape, 0)
    col = lax.broadcasted_iota(jnp.int32, block.shape, 1)
    rows = lax.broadcasted_iota(jnp.int32, (size, 1), 0)
    pivots = jnp.ones((size, 1), jnp.float32)
    for j in range(size):
        pivot = block[j : j + 1, j : j + 1]
        factor = jnp.where(rows > j, block[:, j : j + 1] * (1.0 / pivot), 0.0)
        pivots = jnp.where(rows == j, pivot, pivots)
        line = jnp.where(col[0:1] == j, 1.0, block[j : j + 1, :])
        block = jnp.where((col == j) & (row != j), 0.0, block) - factor * line
    unit = jnp.where(col == row, 1.0, jnp.where(col < row, block, 0.0))
    return unit * lax.rsqrt(pivots)


def factor_kernel(gram_ref, far_ref, out_ref, work):
    size = gram_ref.shape[0]
    work[...] = gram_ref[...] + far_ref[...]
    for start in range(0, size, BLOCK):
        stop = start + BLOCK
        corner = inverse_factor(work[start:stop, start:stop])
        lane = lax.broadcasted_iota(jnp.int32, (BLOCK, size), 1)
        wide = jnp.concatenate(
            [jnp.zeros((BLOCK, start), jnp.float32)] * (start > 0)
            + [corner]
            + [jnp.zeros((BLOCK, size - stop), jnp.float32)] * (stop < size),
            axis=1,
        )
        lines = small_dot(corner, work[start:stop, :], ((1,), (0,)))
        lines = jnp.where((lane >= start) & (lane < stop), wide, lines)
        out_ref[start:stop, :] = jnp.where(lane < stop, lines, 0.0)
        if stop < size:
            factor = small_dot(work[stop:, start:stop], corner, ((1,), (1,)))
            lane = lax.broadcasted_iota(jnp.int32, (size - stop, size), 1)
            old = jnp.where((lane >= start) & (lane < stop), 0.0, work[stop:, :])
            work[stop:, :] = old - small_dot(factor, lines, ((1,), (0,)))


def inverse_cholesky(gram, far):
    whole = pl.BlockSpec(memory_space=pltpu.VMEM)
    return pl.pallas_call(
        factor_kernel,
        out_shape=jax.ShapeDtypeStruct(gram.shape, jnp.float32),
        in_specs=[whole, whole],
        out_specs=whole,
        scratch_shapes=[pltpu.VMEM(gram.shape, jnp.float32)],
        compiler_params=pltpu.CompilerParams(vmem_limit_bytes=16 << 20),
        cost_estimate=LIGHT,
    )(gram, far)


def after(values, *earlier):
    out = lax.optimization_barrier(tuple(values) + earlier)
    return out[: len(values)]


def exchanged(texture, sketch):
    col, row = lax.axis_index("cols"), lax.axis_index("rows")
    bits = lax.rem(col, 2), lax.rem(lax.div(col, 2), 2)
    side = jnp.where(row == 0, bits[0], bits[1])
    odd = jnp.where(row == 0, bits[1], bits[0])

    def pairs(first_core, second_core):
        return [(8 * r + c, 8 * r + (c ^ step)) for r, step in ((0, first_core), (1, second_core)) for c in range(8)]

    outer, inner, line = pairs(1, 2), pairs(2, 1), pairs(4, 4)
    chunks = range(len(SIZES))
    starts = [4 * sum(SIZES[:k]) for k in chunks]
    last = [None]

    def send(x, targets):
        last[0] = x
        return lax.ppermute(x, ("rows", "cols"), targets)

    def rows_of(k, which):
        return lax.dynamic_slice_in_dim(texture, starts[k] + which * (2 * SIZES[k]), 2 * SIZES[k])

    def part(x, which):
        return lax.dynamic_slice_in_dim(x, which * (x.shape[0] // 2), x.shape[0] // 2)

    def joined(own, other):
        return jnp.where(odd == 0, jnp.concatenate([own, other]), jnp.concatenate([other, own]))

    arriving, own = {}, {}
    pinned = [pltpu.with_memory_space_constraint(x, pltpu.HBM) for x in (texture, sketch)]

    def matmuls(group):
        chosen = [(k, 1 - side if theirs else side) for k, theirs in group]
        parts = [(starts[k] + which * (2 * SIZES[k]), 2 * SIZES[k]) for k, which in chosen]
        made = sketched(*pinned, parts, [] if last[0] is None else [last[0]])
        last[0] = made[0]
        for (k, theirs), image in zip(group, made):
            if theirs:
                arriving[k] = lax.ppermute(image, ("rows", "cols"), outer)
            else:
                own[k] = image

    kept, half, sums = {}, {}, [()]

    def arrived(k):
        return after([arriving[k]], last[0])[0]

    def to_inner(k):
        total = own[k] + arrived(k)
        kept[k] = part(total, odd)
        arriving[k] = send(part(total, 1 - odd), inner)

    def to_line(k):
        kept[k] = kept[k] + arrived(k)
        arriving[k] = send(kept[k], line)

    def back_to_inner(k):
        kept[k] = kept[k] + arrived(k)
        arriving[k] = send(kept[k], inner)

    def back_to_outer(k):
        half[k] = joined(kept[k], arrived(k))
        arriving[k] = send(half[k], outer)

    def gather(rows, image):
        terms = inner_rows(image, image), inner_rows(image, rows)
        sums[0] = lax.optimization_barrier(tuple(map(jnp.add, sums[0], terms)) if sums[0] else terms)
        last[0] = sums[0][0]

    def gather_own(k):
        gather(rows_of(k, side), *after([half[k]], last[0]))

    def gather_far(k):
        gather(rows_of(k, 1 - side), arrived(k))

    steps = dict(i=to_inner, l=to_line, b=back_to_inner, o=back_to_outer, g=gather_own, f=gather_far, m=matmuls)
    for name, k in STEPS:
        steps[name](k)
    return sums[0]


def per_device(texture, sketch):
    if lax.axis_size("cols") == 8 and texture.shape[0] == 4 * sum(SIZES):
        gram, product = exchanged(texture, sketch)
    else:
        partial = jnp.dot(texture, sketch, precision=HIGH, preferred_element_type=jnp.float32)
        image = lax.psum(partial, "cols")
        gram, product = inner_rows(image, image), inner_rows(image, texture)
    pair = [(0, 1), (1, 0)]
    far = lax.ppermute(gram, "rows", pair)
    inverse = inverse_cholesky(gram, far)
    (product,) = after([product], far)
    product = product + lax.ppermute(product, "rows", pair)
    span = gram.shape[0] // lax.axis_size("rows")
    inverse = lax.dynamic_slice_in_dim(inverse, lax.axis_index("rows") * span, span)
    return jnp.dot(inverse, product, precision=HIGH, preferred_element_type=jnp.float32)


def solution(mesh):
    placed = (P(("groups", "rows"), "cols"), P("cols", None))
    return jax.shard_map(
        per_device,
        mesh=mesh,
        in_specs=placed,
        out_specs=P(("groups", "rows"), "cols"),
        check_vma=False,
    )
```

```python
import functools

import jax
import jax.numpy as jnp
from jax import lax
from jax.experimental import pallas as pl
from jax.experimental.pallas import tpu as pltpu
from jax.sharding import PartitionSpec as P

HIGH = lax.Precision.HIGH
STEP = 256
SIZES = (128, 256, 128)
STEPS = [("s", 0, True), ("m", 1, True), ("m", 0, False), ("i", 0), ("m", 2, True), ("l", 0), ("m", 1, False), ("i", 1)]
STEPS += [("m", 2, False), ("i", 2), ("b", 0), ("l", 1), ("l", 2), ("o", 0), ("b", 1), ("w", 0), ("g", 0), ("o", 1), ("b", 2), ("f", 0), ("o", 2)]
STEPS += [("g", 1), ("f", 1), ("g", 2), ("f", 2)]
BLOCK = 64
LIGHT = pl.CostEstimate(flops=1000, bytes_accessed=1000, transcendentals=0)


def split(x):
    high = x.astype(jnp.bfloat16)
    return high, (x - high.astype(jnp.float32)).astype(jnp.bfloat16)


def three_passes(left, right):
    (left_high, left_low), (right_high, right_low) = left, right
    dot = lambda x, y: jnp.dot(x, y, preferred_element_type=jnp.float32)
    return dot(left_high, right_high) + (dot(left_low, right_high) + dot(left_high, right_low))


def sketch_kernel(starts_ref, texture_ref, sketch_ref, *rest):
    outs, (blocks, sketch, sems) = rest[:-3], rest[-3:]
    count = blocks.shape[0]
    fetch = [pltpu.make_async_copy(sketch_ref, sketch, sems.at[count])]
    for k in range(count):
        start = pl.multiple_of(starts_ref[k], STEP)
        fetch.append(pltpu.make_async_copy(texture_ref.at[pl.ds(start, STEP), :], blocks.at[k], sems.at[k]))
    for copy in fetch:
        copy.start()
    fetch[0].wait()
    weights = split(sketch[...])
    k = 0
    for out in outs:
        for row in range(0, out.shape[0], STEP):
            fetch[k + 1].wait()
            out[row : row + STEP, :] = three_passes(split(blocks[k]), weights)
            k += 1


def sketched(texture, sketch, parts, earlier):
    starts = [first + row for first, length in parts for row in range(0, length, STEP)]
    (starts,) = after([jnp.stack(starts).astype(jnp.int32)], *earlier)
    count, (scans, rank) = starts.shape[0], sketch.shape
    there = pl.BlockSpec(memory_space=pl.ANY)
    return pl.pallas_call(
        sketch_kernel,
        out_shape=[jax.ShapeDtypeStruct((length, rank), jnp.float32) for _, length in parts],
        in_specs=[pl.BlockSpec(memory_space=pltpu.SMEM), there, there],
        out_specs=[pl.BlockSpec(memory_space=pltpu.VMEM)] * len(parts),
        scratch_shapes=[
            pltpu.VMEM((count, STEP, scans), jnp.float32),
            pltpu.VMEM((scans, rank), jnp.float32),
            pltpu.SemaphoreType.DMA((count + 1,)),
        ],
        compiler_params=pltpu.CompilerParams(vmem_limit_bytes=16 << 20),
        cost_estimate=pl.CostEstimate(
            flops=6 * count * STEP * scans * rank, bytes_accessed=4 * scans * (count * STEP + rank), transcendentals=0
        ),
    )(starts, texture, sketch)


def inner_rows(left, right):
    return lax.dot_general(
        left,
        right,
        (((0,), (0,)), ((), ())),
        precision=HIGH,
        preferred_element_type=jnp.float32,
    )


def small_dot(left, right, dims):
    return lax.dot_general(
        left,
        right,
        (dims, ((), ())),
        precision=lax.Precision.HIGHEST,
        preferred_element_type=jnp.float32,
    )


def inverse_factor(block):
    size = block.shape[0]
    row = lax.broadcasted_iota(jnp.int32, block.shape, 0)
    col = lax.broadcasted_iota(jnp.int32, block.shape, 1)
    rows = lax.broadcasted_iota(jnp.int32, (size, 1), 0)
    pivots = jnp.ones((size, 1), jnp.float32)
    for j in range(size):
        pivot = block[j : j + 1, j : j + 1]
        factor = jnp.where(rows > j, block[:, j : j + 1] * (1.0 / pivot), 0.0)
        pivots = jnp.where(rows == j, pivot, pivots)
        line = jnp.where(col[0:1] == j, 1.0, block[j : j + 1, :])
        block = jnp.where((col == j) & (row != j), 0.0, block) - factor * line
    unit = jnp.where(col == row, 1.0, jnp.where(col < row, block, 0.0))
    return unit * lax.rsqrt(pivots)


def factor_kernel(gram_ref, far_ref, out_ref, work):
    size = gram_ref.shape[0]
    work[...] = gram_ref[...] + far_ref[...]
    for start in range(0, size, BLOCK):
        stop = start + BLOCK
        corner = inverse_factor(work[start:stop, start:stop])
        lane = lax.broadcasted_iota(jnp.int32, (BLOCK, size), 1)
        wide = jnp.concatenate(
            [jnp.zeros((BLOCK, start), jnp.float32)] * (start > 0)
            + [corner]
            + [jnp.zeros((BLOCK, size - stop), jnp.float32)] * (stop < size),
            axis=1,
        )
        lines = small_dot(corner, work[start:stop, :], ((1,), (0,)))
        lines = jnp.where((lane >= start) & (lane < stop), wide, lines)
        out_ref[start:stop, :] = jnp.where(lane < stop, lines, 0.0)
        if stop < size:
            factor = small_dot(work[stop:, start:stop], corner, ((1,), (1,)))
            lane = lax.broadcasted_iota(jnp.int32, (size - stop, size), 1)
            old = jnp.where((lane >= start) & (lane < stop), 0.0, work[stop:, :])
            work[stop:, :] = old - small_dot(factor, lines, ((1,), (0,)))


def inverse_cholesky(gram, far):
    whole = pl.BlockSpec(memory_space=pltpu.VMEM)
    return pl.pallas_call(
        factor_kernel,
        out_shape=jax.ShapeDtypeStruct(gram.shape, jnp.float32),
        in_specs=[whole, whole],
        out_specs=whole,
        scratch_shapes=[pltpu.VMEM(gram.shape, jnp.float32)],
        compiler_params=pltpu.CompilerParams(vmem_limit_bytes=16 << 20),
        cost_estimate=LIGHT,
    )(gram, far)


def after(values, *earlier):
    out = lax.optimization_barrier(tuple(values) + earlier)
    return out[: len(values)]


def exchanged(texture, sketch):
    col, row = lax.axis_index("cols"), lax.axis_index("rows")
    bits = lax.rem(col, 2), lax.rem(lax.div(col, 2), 2)
    side = jnp.where(row == 0, bits[0], bits[1])
    odd = jnp.where(row == 0, bits[1], bits[0])

    def pairs(first_core, second_core):
        return [(8 * r + c, 8 * r + (c ^ step)) for r, step in ((0, first_core), (1, second_core)) for c in range(8)]

    outer, inner, line = pairs(1, 2), pairs(2, 1), pairs(4, 4)
    chunks = range(len(SIZES))
    starts = [4 * sum(SIZES[:k]) for k in chunks]
    last = [None]

    def send(x, targets):
        last[0] = x
        return lax.ppermute(x, ("rows", "cols"), targets)

    def rows_of(k, which):
        return lax.dynamic_slice_in_dim(texture, starts[k] + which * (2 * SIZES[k]), 2 * SIZES[k])

    def part(x, which):
        return lax.dynamic_slice_in_dim(x, which * (x.shape[0] // 2), x.shape[0] // 2)

    def joined(own, other):
        return jnp.where(odd == 0, jnp.concatenate([own, other]), jnp.concatenate([other, own]))

    arriving, own = {}, {}

    def placed(k, theirs, image):
        last[0] = image
        if theirs:
            arriving[k] = lax.ppermute(image, ("rows", "cols"), outer)
        else:
            own[k] = image

    def first_matmul(k, theirs):
        pinned = [pltpu.with_memory_space_constraint(x, pltpu.HBM) for x in (texture, sketch)]
        which = 1 - side if theirs else side
        parts = [(starts[k] + which * (2 * SIZES[k]), 2 * SIZES[k])]
        placed(k, theirs, sketched(*pinned, parts, [])[0])

    def matmul(k, theirs):
        (weights,) = after([sketch], last[0])
        rows = rows_of(k, 1 - side if theirs else side)
        placed(k, theirs, jnp.dot(rows, weights, precision=HIGH, preferred_element_type=jnp.float32))

    kept, half, sums = {}, {}, [()]

    def arrived(k):
        return after([arriving[k]], last[0])[0]

    def to_inner(k):
        total = own[k] + arrived(k)
        kept[k] = part(total, odd)
        arriving[k] = send(part(total, 1 - odd), inner)

    def to_line(k):
        kept[k] = kept[k] + arrived(k)
        arriving[k] = send(kept[k], line)

    def back_to_inner(k):
        kept[k] = kept[k] + arrived(k)
        arriving[k] = send(kept[k], inner)

    def back_to_outer(k):
        half[k] = joined(kept[k], arrived(k))
        arriving[k] = send(half[k], outer)

    def gather(rows, image):
        terms = inner_rows(image, image), inner_rows(image, rows)
        sums[0] = lax.optimization_barrier(tuple(map(jnp.add, sums[0], terms)) if sums[0] else terms)
        last[0] = sums[0][0]

    def gather_own(k):
        gather(rows_of(k, side), *after([half[k]], last[0]))

    def wait_far(k):
        arriving[k] = last[0] = arrived(k)

    def gather_far(k):
        gather(rows_of(k, 1 - side), arrived(k))

    steps = dict(i=to_inner, l=to_line, b=back_to_inner, o=back_to_outer, g=gather_own, f=gather_far, w=wait_far, s=first_matmul, m=matmul)
    for name, *chunk in STEPS:
        steps[name](*chunk)
    return sums[0]


def per_device(texture, sketch):
    if lax.axis_size("cols") == 8 and texture.shape[0] == 4 * sum(SIZES):
        gram, product = exchanged(texture, sketch)
    else:
        partial = jnp.dot(texture, sketch, precision=HIGH, preferred_element_type=jnp.float32)
        image = lax.psum(partial, "cols")
        gram, product = inner_rows(image, image), inner_rows(image, texture)
    pair = [(0, 1), (1, 0)]
    far = lax.ppermute(gram, "rows", pair)
    inverse = inverse_cholesky(gram, far)
    (product,) = after([product], far)
    product = product + lax.ppermute(product, "rows", pair)
    span = gram.shape[0] // lax.axis_size("rows")
    inverse = lax.dynamic_slice_in_dim(inverse, lax.axis_index("rows") * span, span)
    return jnp.dot(inverse, product, precision=HIGH, preferred_element_type=jnp.float32)


def solution(mesh):
    placed = (P(("groups", "rows"), "cols"), P("cols", None))
    return jax.shard_map(
        per_device,
        mesh=mesh,
        in_specs=placed,
        out_specs=P(("groups", "rows"), "cols"),
        check_vma=False,
    )
```

```python
import functools

import jax
import jax.numpy as jnp
from jax import lax
from jax.experimental import pallas as pl
from jax.experimental.pallas import tpu as pltpu
from jax.sharding import PartitionSpec as P

HIGH = lax.Precision.HIGH
STEP = 256
SIZES = (128, 256, 128)
STEPS = [("s", 0, True), ("m", 1, True), ("m", 0, False), ("i", 0), ("m", 2, True), ("l", 0), ("m", 1, False), ("i", 1)]
STEPS += [("m", 2, False), ("i", 2), ("b", 0), ("l", 1), ("l", 2), ("o", 0), ("b", 1), ("w", 0), ("g", 0), ("o", 1), ("b", 2), ("f", 0), ("o", 2)]
STEPS += [("g", 1), ("f", 1), ("g", 2), ("f", 2)]
BLOCK = 64
TILE = 8
LIGHT = pl.CostEstimate(flops=1000, bytes_accessed=1000, transcendentals=0)


def split(x):
    high = x.astype(jnp.bfloat16)
    return high, (x - high.astype(jnp.float32)).astype(jnp.bfloat16)


def three_passes(left, right):
    (left_high, left_low), (right_high, right_low) = left, right
    dot = lambda x, y: jnp.dot(x, y, preferred_element_type=jnp.float32)
    return dot(left_high, right_high) + (dot(left_low, right_high) + dot(left_high, right_low))


def sketch_kernel(starts_ref, texture_ref, sketch_ref, *rest):
    outs, (blocks, sketch, sems) = rest[:-3], rest[-3:]
    count = blocks.shape[0]
    fetch = [pltpu.make_async_copy(sketch_ref, sketch, sems.at[count])]
    for k in range(count):
        start = pl.multiple_of(starts_ref[k], STEP)
        fetch.append(pltpu.make_async_copy(texture_ref.at[pl.ds(start, STEP), :], blocks.at[k], sems.at[k]))
    for copy in fetch:
        copy.start()
    fetch[0].wait()
    weights = split(sketch[...])
    k = 0
    for out in outs:
        for row in range(0, out.shape[0], STEP):
            fetch[k + 1].wait()
            out[row : row + STEP, :] = three_passes(split(blocks[k]), weights)
            k += 1


def sketched(texture, sketch, parts, earlier):
    starts = [first + row for first, length in parts for row in range(0, length, STEP)]
    (starts,) = after([jnp.stack(starts).astype(jnp.int32)], *earlier)
    count, (scans, rank) = starts.shape[0], sketch.shape
    there = pl.BlockSpec(memory_space=pl.ANY)
    return pl.pallas_call(
        sketch_kernel,
        out_shape=[jax.ShapeDtypeStruct((length, rank), jnp.float32) for _, length in parts],
        in_specs=[pl.BlockSpec(memory_space=pltpu.SMEM), there, there],
        out_specs=[pl.BlockSpec(memory_space=pltpu.VMEM)] * len(parts),
        scratch_shapes=[
            pltpu.VMEM((count, STEP, scans), jnp.float32),
            pltpu.VMEM((scans, rank), jnp.float32),
            pltpu.SemaphoreType.DMA((count + 1,)),
        ],
        compiler_params=pltpu.CompilerParams(vmem_limit_bytes=16 << 20),
        cost_estimate=pl.CostEstimate(
            flops=6 * count * STEP * scans * rank, bytes_accessed=4 * scans * (count * STEP + rank), transcendentals=0
        ),
    )(starts, texture, sketch)


def inner_rows(left, right):
    return lax.dot_general(
        left,
        right,
        (((0,), (0,)), ((), ())),
        precision=HIGH,
        preferred_element_type=jnp.float32,
    )


def small_dot(left, right, dims):
    return lax.dot_general(
        left,
        right,
        (dims, ((), ())),
        precision=lax.Precision.HIGHEST,
        preferred_element_type=jnp.float32,
    )


def inverse_factor(block):
    size = block.shape[0]
    sub = lax.broadcasted_iota(jnp.int32, (TILE, size), 0)
    lane = lax.broadcasted_iota(jnp.int32, (TILE, size), 1)
    along = lambda x, l: jnp.broadcast_to(x[:, l : l + 1], (TILE, size))
    down = lambda x, j: jnp.broadcast_to(x[j : j + 1, :], (TILE, size))
    tiles = [block[row : row + TILE, :] for row in range(0, size, TILE)]
    outs = []
    for s, lines in enumerate(tiles):
        low = s * TILE
        inside = (lane >= low) & (lane < low + TILE)
        corner = [along(lines, low + c) for c in range(TILE)]
        lines = jnp.where(inside, jnp.where(lane - low == sub, 1.0, 0.0), lines)
        out = jnp.zeros((TILE, size), jnp.float32)
        scale = jnp.ones((TILE, size), jnp.float32)
        for j in range(TILE):
            pivot = down(corner[j], j)
            inverse = 1.0 / pivot
            factor = jnp.where(sub == j, 0.0, corner[j] * inverse)
            scale = jnp.where(sub == j, inverse, scale)
            line = down(lines, j)
            out = jnp.where(sub == j, line * lax.rsqrt(pivot), out)
            for c in range(j + 1, TILE):
                corner[c] = corner[c] - factor * down(corner[c], j)
            lines = lines - factor * line
        outs.append(jnp.where(lane < low + TILE, out, 0.0))
        lines = lines * scale
        rows = [down(lines, c) for c in range(TILE)]
        for t in range(s + 1, len(tiles)):
            term = along(tiles[t], low) * rows[0]
            for c in range(1, TILE):
                term = term + along(tiles[t], low + c) * rows[c]
            tiles[t] = jnp.where(inside, 0.0, tiles[t]) - term
    return jnp.concatenate(outs, axis=0)


def factor_kernel(gram_ref, far_ref, out_ref, work):
    size = gram_ref.shape[0]
    work[...] = gram_ref[...] + far_ref[...]
    for start in range(0, size, BLOCK):
        stop = start + BLOCK
        corner = inverse_factor(work[start:stop, start:stop])
        lane = lax.broadcasted_iota(jnp.int32, (BLOCK, size), 1)
        wide = jnp.concatenate(
            [jnp.zeros((BLOCK, start), jnp.float32)] * (start > 0)
            + [corner]
            + [jnp.zeros((BLOCK, size - stop), jnp.float32)] * (stop < size),
            axis=1,
        )
        lines = small_dot(corner, work[start:stop, :], ((1,), (0,)))
        lines = jnp.where((lane >= start) & (lane < stop), wide, lines)
        out_ref[start:stop, :] = jnp.where(lane < stop, lines, 0.0)
        if stop < size:
            factor = small_dot(work[stop:, start:stop], corner, ((1,), (1,)))
            lane = lax.broadcasted_iota(jnp.int32, (size - stop, size), 1)
            old = jnp.where((lane >= start) & (lane < stop), 0.0, work[stop:, :])
            work[stop:, :] = old - small_dot(factor, lines, ((1,), (0,)))


def inverse_cholesky(gram, far):
    whole = pl.BlockSpec(memory_space=pltpu.VMEM)
    return pl.pallas_call(
        factor_kernel,
        out_shape=jax.ShapeDtypeStruct(gram.shape, jnp.float32),
        in_specs=[whole, whole],
        out_specs=whole,
        scratch_shapes=[pltpu.VMEM(gram.shape, jnp.float32)],
        compiler_params=pltpu.CompilerParams(vmem_limit_bytes=16 << 20),
        cost_estimate=LIGHT,
    )(gram, far)


def after(values, *earlier):
    out = lax.optimization_barrier(tuple(values) + earlier)
    return out[: len(values)]


def exchanged(texture, sketch):
    col, row = lax.axis_index("cols"), lax.axis_index("rows")
    bits = lax.rem(col, 2), lax.rem(lax.div(col, 2), 2)
    side = jnp.where(row == 0, bits[0], bits[1])
    odd = jnp.where(row == 0, bits[1], bits[0])

    def pairs(first_core, second_core):
        return [(8 * r + c, 8 * r + (c ^ step)) for r, step in ((0, first_core), (1, second_core)) for c in range(8)]

    outer, inner, line = pairs(1, 2), pairs(2, 1), pairs(4, 4)
    chunks = range(len(SIZES))
    starts = [4 * sum(SIZES[:k]) for k in chunks]
    last = [None]

    def send(x, targets):
        last[0] = x
        return lax.ppermute(x, ("rows", "cols"), targets)

    def rows_of(k, which):
        return lax.dynamic_slice_in_dim(texture, starts[k] + which * (2 * SIZES[k]), 2 * SIZES[k])

    def part(x, which):
        return lax.dynamic_slice_in_dim(x, which * (x.shape[0] // 2), x.shape[0] // 2)

    def joined(own, other):
        return jnp.where(odd == 0, jnp.concatenate([own, other]), jnp.concatenate([other, own]))

    arriving, own = {}, {}

    def placed(k, theirs, image):
        last[0] = image
        if theirs:
            arriving[k] = lax.ppermute(image, ("rows", "cols"), outer)
        else:
            own[k] = image

    def first_matmul(k, theirs):
        pinned = [pltpu.with_memory_space_constraint(x, pltpu.HBM) for x in (texture, sketch)]
        which = 1 - side if theirs else side
        parts = [(starts[k] + which * (2 * SIZES[k]), 2 * SIZES[k])]
        placed(k, theirs, sketched(*pinned, parts, [])[0])

    def matmul(k, theirs):
        (weights,) = after([sketch], last[0])
        rows = rows_of(k, 1 - side if theirs else side)
        placed(k, theirs, jnp.dot(rows, weights, precision=HIGH, preferred_element_type=jnp.float32))

    kept, half, sums = {}, {}, [()]

    def arrived(k):
        return after([arriving[k]], last[0])[0]

    def to_inner(k):
        total = own[k] + arrived(k)
        kept[k] = part(total, odd)
        arriving[k] = send(part(total, 1 - odd), inner)

    def to_line(k):
        kept[k] = kept[k] + arrived(k)
        arriving[k] = send(kept[k], line)

    def back_to_inner(k):
        kept[k] = kept[k] + arrived(k)
        arriving[k] = send(kept[k], inner)

    def back_to_outer(k):
        half[k] = joined(kept[k], arrived(k))
        arriving[k] = send(half[k], outer)

    def gather(rows, image):
        terms = inner_rows(image, image), inner_rows(image, rows)
        sums[0] = lax.optimization_barrier(tuple(map(jnp.add, sums[0], terms)) if sums[0] else terms)
        last[0] = sums[0][0]

    def gather_own(k):
        gather(rows_of(k, side), *after([half[k]], last[0]))

    def wait_far(k):
        arriving[k] = last[0] = arrived(k)

    def gather_far(k):
        gather(rows_of(k, 1 - side), arrived(k))

    steps = dict(i=to_inner, l=to_line, b=back_to_inner, o=back_to_outer, g=gather_own, f=gather_far, w=wait_far, s=first_matmul, m=matmul)
    for name, *chunk in STEPS:
        steps[name](*chunk)
    return sums[0]


def per_device(texture, sketch):
    if lax.axis_size("cols") == 8 and texture.shape[0] == 4 * sum(SIZES):
        gram, product = exchanged(texture, sketch)
    else:
        partial = jnp.dot(texture, sketch, precision=HIGH, preferred_element_type=jnp.float32)
        image = lax.psum(partial, "cols")
        gram, product = inner_rows(image, image), inner_rows(image, texture)
    pair = [(0, 1), (1, 0)]
    far = lax.ppermute(gram, "rows", pair)
    inverse = inverse_cholesky(gram, far)
    (product,) = after([product], far)
    product = product + lax.ppermute(product, "rows", pair)
    span = gram.shape[0] // lax.axis_size("rows")
    inverse = lax.dynamic_slice_in_dim(inverse, lax.axis_index("rows") * span, span)
    return jnp.dot(inverse, product, precision=HIGH, preferred_element_type=jnp.float32)


def solution(mesh):
    placed = (P(("groups", "rows"), "cols"), P("cols", None))
    return jax.shard_map(
        per_device,
        mesh=mesh,
        in_specs=placed,
        out_specs=P(("groups", "rows"), "cols"),
        check_vma=False,
    )
```

```python
import functools

import jax
import jax.numpy as jnp
from jax import lax
from jax.experimental import pallas as pl
from jax.experimental.pallas import tpu as pltpu
from jax.sharding import PartitionSpec as P

HIGH = lax.Precision.HIGH
STEP = 256
SIZES = (128, 256, 128)
CROSSED = (True, True, True)
STEPS = [("s", 0, True), ("m", 1, True), ("m", 0, False), ("i", 0), ("m", 2, True), ("l", 0), ("m", 1, False), ("i", 1)]
STEPS += [("m", 2, False), ("i", 2), ("b", 0), ("l", 1), ("l", 2), ("o", 0), ("b", 1), ("w", 0), ("g", 0), ("o", 1), ("b", 2), ("f", 0), ("o", 2)]
STEPS += [("g", 1), ("f", 1), ("g", 2), ("f", 2)]
BLOCK = 128
TILE = 8
LIGHT = pl.CostEstimate(flops=1000, bytes_accessed=1000, transcendentals=0)


def split(x):
    high = x.astype(jnp.bfloat16)
    return high, (x - high.astype(jnp.float32)).astype(jnp.bfloat16)


def three_passes(left, right):
    (left_high, left_low), (right_high, right_low) = left, right
    dot = lambda x, y: jnp.dot(x, y, preferred_element_type=jnp.float32)
    return dot(left_high, right_high) + (dot(left_low, right_high) + dot(left_high, right_low))


def sketch_kernel(starts_ref, texture_ref, sketch_ref, *rest):
    outs, (blocks, sketch, sems) = rest[:-3], rest[-3:]
    count = blocks.shape[0]
    fetch = [pltpu.make_async_copy(sketch_ref, sketch, sems.at[count])]
    for k in range(count):
        start = pl.multiple_of(starts_ref[k], STEP)
        fetch.append(pltpu.make_async_copy(texture_ref.at[pl.ds(start, STEP), :], blocks.at[k], sems.at[k]))
    for copy in fetch:
        copy.start()
    fetch[0].wait()
    weights = split(sketch[...])
    k = 0
    for out in outs:
        for row in range(0, out.shape[0], STEP):
            fetch[k + 1].wait()
            out[row : row + STEP, :] = three_passes(split(blocks[k]), weights)
            k += 1


def sketched(texture, sketch, parts, earlier):
    starts = [first + row for first, length in parts for row in range(0, length, STEP)]
    (starts,) = after([jnp.stack(starts).astype(jnp.int32)], *earlier)
    count, (scans, rank) = starts.shape[0], sketch.shape
    there = pl.BlockSpec(memory_space=pl.ANY)
    return pl.pallas_call(
        sketch_kernel,
        out_shape=[jax.ShapeDtypeStruct((length, rank), jnp.float32) for _, length in parts],
        in_specs=[pl.BlockSpec(memory_space=pltpu.SMEM), there, there],
        out_specs=[pl.BlockSpec(memory_space=pltpu.VMEM)] * len(parts),
        scratch_shapes=[
            pltpu.VMEM((count, STEP, scans), jnp.float32),
            pltpu.VMEM((scans, rank), jnp.float32),
            pltpu.SemaphoreType.DMA((count + 1,)),
        ],
        compiler_params=pltpu.CompilerParams(vmem_limit_bytes=16 << 20),
        cost_estimate=pl.CostEstimate(
            flops=6 * count * STEP * scans * rank, bytes_accessed=4 * scans * (count * STEP + rank), transcendentals=0
        ),
    )(starts, texture, sketch)


def inner_rows(left, right):
    return lax.dot_general(
        left,
        right,
        (((0,), (0,)), ((), ())),
        precision=HIGH,
        preferred_element_type=jnp.float32,
    )


def small_dot(left, right, dims):
    return lax.dot_general(
        left,
        right,
        (dims, ((), ())),
        precision=lax.Precision.HIGHEST,
        preferred_element_type=jnp.float32,
    )


def inverse_factor(block):
    size = block.shape[0]
    sub = lax.broadcasted_iota(jnp.int32, (TILE, size), 0)
    lane = lax.broadcasted_iota(jnp.int32, (TILE, size), 1)
    along = lambda x, l: jnp.broadcast_to(x[:, l : l + 1], (TILE, size))
    down = lambda x, j: jnp.broadcast_to(x[j : j + 1, :], (TILE, size))
    tiles = [block[row : row + TILE, :] for row in range(0, size, TILE)]
    outs = []
    for s, lines in enumerate(tiles):
        low = s * TILE
        inside = (lane >= low) & (lane < low + TILE)
        corner = [jnp.where(sub < TILE, along(lines, low + c), 0.0) for c in range(TILE)]
        lines = jnp.where(inside, jnp.where(lane - low == sub, 1.0, 0.0), lines)
        out = jnp.zeros((TILE, size), jnp.float32)
        same = jnp.ones((TILE, size), jnp.float32)
        cross = jnp.zeros((TILE, size), jnp.float32)
        for j in range(0, TILE, 2):
            both = (sub == j) | (sub == j + 1)
            left, right = corner[j], corner[j + 1]
            a, b, c = down(left, j), down(right, j), down(right, j + 1)
            inverse = 1.0 / (a * c - b * b)
            a_over, b_over, c_over = a * inverse, b * inverse, c * inverse
            first = jnp.where(both, 0.0, left * c_over - right * b_over)
            second = jnp.where(both, 0.0, right * a_over - left * b_over)
            upper, lower = down(lines, j), down(lines, j + 1)
            root = lax.rsqrt(a)
            ratio = b * (root * root)
            lower_out = (lower - ratio * upper) * lax.rsqrt(c - b * ratio)
            out = jnp.where(sub == j, upper * root, jnp.where(sub == j + 1, lower_out, out))
            same = jnp.where(sub == j, c_over, jnp.where(sub == j + 1, a_over, same))
            cross = jnp.where(both, b_over, cross)
            for k in range(j + 2, TILE):
                corner[k] = corner[k] - (first * down(corner[k], j) + second * down(corner[k], j + 1))
            lines = lines - (first * upper + second * lower)
        outs.append(jnp.where(lane < low + TILE, out, 0.0))
        partner = jnp.where(sub % 2 == 0, pltpu.roll(lines, TILE - 1, 0), pltpu.roll(lines, 1, 0))
        lines = lines * same - cross * partner
        rows = [down(lines, c) for c in range(TILE)]
        for t in range(s + 1, len(tiles)):
            terms = [along(tiles[t], low + c) * rows[c] for c in range(TILE)]
            while len(terms) > 1:
                terms = [x + y for x, y in zip(terms[::2], terms[1::2])]
            tiles[t] = jnp.where(inside, 0.0, tiles[t]) - terms[0]
    return jnp.concatenate(outs, axis=0)


def factor_kernel(gram_ref, far_ref, out_ref, work):
    size = gram_ref.shape[0]
    work[...] = gram_ref[...] + far_ref[...]
    for start in range(0, size, BLOCK):
        stop = start + BLOCK
        corner = inverse_factor(work[start:stop, start:stop])
        lane = lax.broadcasted_iota(jnp.int32, (BLOCK, size), 1)
        wide = jnp.concatenate(
            [jnp.zeros((BLOCK, start), jnp.float32)] * (start > 0)
            + [corner]
            + [jnp.zeros((BLOCK, size - stop), jnp.float32)] * (stop < size),
            axis=1,
        )
        lines = small_dot(corner, work[start:stop, :], ((1,), (0,)))
        lines = jnp.where((lane >= start) & (lane < stop), wide, lines)
        out_ref[start:stop, :] = jnp.where(lane < stop, lines, 0.0)
        if stop < size:
            factor = small_dot(work[stop:, start:stop], corner, ((1,), (1,)))
            lane = lax.broadcasted_iota(jnp.int32, (size - stop, size), 1)
            old = jnp.where((lane >= start) & (lane < stop), 0.0, work[stop:, :])
            work[stop:, :] = old - small_dot(factor, lines, ((1,), (0,)))


def inverse_cholesky(gram, far):
    whole = pl.BlockSpec(memory_space=pltpu.VMEM)
    return pl.pallas_call(
        factor_kernel,
        out_shape=jax.ShapeDtypeStruct(gram.shape, jnp.float32),
        in_specs=[whole, whole],
        out_specs=whole,
        scratch_shapes=[pltpu.VMEM(gram.shape, jnp.float32)],
        compiler_params=pltpu.CompilerParams(vmem_limit_bytes=16 << 20),
        cost_estimate=LIGHT,
    )(gram, far)


def after(values, *earlier):
    out = lax.optimization_barrier(tuple(values) + earlier)
    return out[: len(values)]


def exchanged(texture, sketch):
    col, row = lax.axis_index("cols"), lax.axis_index("rows")
    bits = lax.rem(col, 2), lax.rem(lax.div(col, 2), 2)

    def pairs(first_core, second_core):
        return [(8 * r + c, 8 * r + (c ^ step)) for r, step in ((0, first_core), (1, second_core)) for c in range(8)]

    line = pairs(4, 4)
    outer = [pairs(1, 2 if crossed else 1) for crossed in CROSSED]
    inner = [pairs(2, 1 if crossed else 2) for crossed in CROSSED]
    side = [jnp.where(row == 0, bits[0], bits[1]) if crossed else bits[0] for crossed in CROSSED]
    odd = [jnp.where(row == 0, bits[1], bits[0]) if crossed else bits[1] for crossed in CROSSED]
    chunks = range(len(SIZES))
    starts = [4 * sum(SIZES[:k]) for k in chunks]
    last = [None]

    def send(x, targets):
        last[0] = x
        return lax.ppermute(x, ("rows", "cols"), targets)

    def rows_of(k, which):
        return lax.dynamic_slice_in_dim(texture, starts[k] + which * (2 * SIZES[k]), 2 * SIZES[k])

    def part(x, which):
        return lax.dynamic_slice_in_dim(x, which * (x.shape[0] // 2), x.shape[0] // 2)

    def joined(k, own, other):
        return jnp.where(odd[k] == 0, jnp.concatenate([own, other]), jnp.concatenate([other, own]))

    arriving, own = {}, {}

    def placed(k, theirs, image):
        last[0] = image
        if theirs:
            arriving[k] = lax.ppermute(image, ("rows", "cols"), outer[k])
        else:
            own[k] = image

    def first_matmul(k, theirs):
        pinned = [pltpu.with_memory_space_constraint(x, pltpu.HBM) for x in (texture, sketch)]
        which = 1 - side[k] if theirs else side[k]
        parts = [(starts[k] + which * (2 * SIZES[k]), 2 * SIZES[k])]
        placed(k, theirs, sketched(*pinned, parts, [])[0])

    def matmul(k, theirs):
        (weights,) = after([sketch], last[0])
        rows = rows_of(k, 1 - side[k] if theirs else side[k])
        placed(k, theirs, jnp.dot(rows, weights, precision=HIGH, preferred_element_type=jnp.float32))

    kept, half, sums = {}, {}, [()]

    def arrived(k):
        return after([arriving[k]], last[0])[0]

    def to_inner(k):
        total = own[k] + arrived(k)
        kept[k] = part(total, odd[k])
        arriving[k] = send(part(total, 1 - odd[k]), inner[k])

    def to_line(k):
        kept[k] = kept[k] + arrived(k)
        arriving[k] = send(kept[k], line)

    def back_to_inner(k):
        kept[k] = kept[k] + arrived(k)
        arriving[k] = send(kept[k], inner[k])

    def back_to_outer(k):
        half[k] = joined(k, kept[k], arrived(k))
        arriving[k] = send(half[k], outer[k])

    def gather(rows, image):
        terms = inner_rows(image, image), inner_rows(image, rows)
        sums[0] = lax.optimization_barrier(tuple(map(jnp.add, sums[0], terms)) if sums[0] else terms)
        last[0] = sums[0][0]

    def gather_own(k):
        gather(rows_of(k, side[k]), *after([half[k]], last[0]))

    def wait_far(k):
        arriving[k] = last[0] = arrived(k)

    def gather_far(k):
        gather(rows_of(k, 1 - side[k]), arrived(k))

    steps = dict(i=to_inner, l=to_line, b=back_to_inner, o=back_to_outer, g=gather_own, f=gather_far, w=wait_far, s=first_matmul, m=matmul)
    for name, *chunk in STEPS:
        steps[name](*chunk)
    return sums[0]


def per_device(texture, sketch):
    if lax.axis_size("cols") == 8 and texture.shape[0] == 4 * sum(SIZES):
        gram, product = exchanged(texture, sketch)
    else:
        partial = jnp.dot(texture, sketch, precision=HIGH, preferred_element_type=jnp.float32)
        image = lax.psum(partial, "cols")
        gram, product = inner_rows(image, image), inner_rows(image, texture)
    pair = [(0, 1), (1, 0)]
    far = lax.ppermute(gram, "rows", pair)
    inverse = inverse_cholesky(gram, far)
    (product,) = after([product], far)
    product = product + lax.ppermute(product, "rows", pair)
    span = gram.shape[0] // lax.axis_size("rows")
    inverse = lax.dynamic_slice_in_dim(inverse, lax.axis_index("rows") * span, span)
    return jnp.dot(inverse, product, precision=HIGH, preferred_element_type=jnp.float32)


def solution(mesh):
    placed = (P(("groups", "rows"), "cols"), P("cols", None))
    return jax.shard_map(
        per_device,
        mesh=mesh,
        in_specs=placed,
        out_specs=P(("groups", "rows"), "cols"),
        check_vma=False,
    )
```

```python
import functools

import jax
import jax.numpy as jnp
from jax import lax
from jax.experimental import pallas as pl
from jax.experimental.pallas import tpu as pltpu
from jax.sharding import PartitionSpec as P

HIGH = lax.Precision.HIGH
STEP = 256
SIZES = (128, 256, 128)
CROSSED = (True, True, True)
STEPS = [("s", 0, True), ("m", 1, True), ("m", 0, False), ("i", 0), ("m", 2, True), ("m", 1, False), ("l", 0), ("i", 1)]
STEPS += [("m", 2, False), ("i", 2), ("b", 0), ("l", 1), ("l", 2), ("b", 1), ("o", 0), ("w", 0), ("g", 0), ("o", 1), ("b", 2), ("f", 0), ("o", 2)]
STEPS += [("g", 1), ("f", 1), ("g", 2), ("f", 2)]
BLOCK = 128
TILE = 8
LIGHT = pl.CostEstimate(flops=1000, bytes_accessed=1000, transcendentals=0)


def split(x):
    high = x.astype(jnp.bfloat16)
    return high, (x - high.astype(jnp.float32)).astype(jnp.bfloat16)


def three_passes(left, right):
    (left_high, left_low), (right_high, right_low) = left, right
    dot = lambda x, y: jnp.dot(x, y, preferred_element_type=jnp.float32)
    return dot(left_high, right_high) + (dot(left_low, right_high) + dot(left_high, right_low))


def sketch_kernel(starts_ref, texture_ref, sketch_ref, *rest):
    outs, (blocks, sketch, sems) = rest[:-3], rest[-3:]
    count = blocks.shape[0]
    fetch = [pltpu.make_async_copy(sketch_ref, sketch, sems.at[count])]
    for k in range(count):
        start = pl.multiple_of(starts_ref[k], STEP)
        fetch.append(pltpu.make_async_copy(texture_ref.at[pl.ds(start, STEP), :], blocks.at[k], sems.at[k]))
    for copy in fetch:
        copy.start()
    fetch[0].wait()
    weights = split(sketch[...])
    k = 0
    for out in outs:
        for row in range(0, out.shape[0], STEP):
            fetch[k + 1].wait()
            out[row : row + STEP, :] = three_passes(split(blocks[k]), weights)
            k += 1


def sketched(texture, sketch, parts, earlier):
    starts = [first + row for first, length in parts for row in range(0, length, STEP)]
    (starts,) = after([jnp.stack(starts).astype(jnp.int32)], *earlier)
    count, (scans, rank) = starts.shape[0], sketch.shape
    there = pl.BlockSpec(memory_space=pl.ANY)
    return pl.pallas_call(
        sketch_kernel,
        out_shape=[jax.ShapeDtypeStruct((length, rank), jnp.float32) for _, length in parts],
        in_specs=[pl.BlockSpec(memory_space=pltpu.SMEM), there, there],
        out_specs=[pl.BlockSpec(memory_space=pltpu.VMEM)] * len(parts),
        scratch_shapes=[
            pltpu.VMEM((count, STEP, scans), jnp.float32),
            pltpu.VMEM((scans, rank), jnp.float32),
            pltpu.SemaphoreType.DMA((count + 1,)),
        ],
        compiler_params=pltpu.CompilerParams(vmem_limit_bytes=16 << 20),
        cost_estimate=pl.CostEstimate(
            flops=6 * count * STEP * scans * rank, bytes_accessed=4 * scans * (count * STEP + rank), transcendentals=0
        ),
    )(starts, texture, sketch)


def inner_rows(left, right):
    return lax.dot_general(
        left,
        right,
        (((0,), (0,)), ((), ())),
        precision=HIGH,
        preferred_element_type=jnp.float32,
    )


def small_dot(left, right, dims):
    return lax.dot_general(
        left,
        right,
        (dims, ((), ())),
        precision=lax.Precision.HIGHEST,
        preferred_element_type=jnp.float32,
    )


def inverse_factor(block):
    size = block.shape[0]
    sub = lax.broadcasted_iota(jnp.int32, (TILE, size), 0)
    lane = lax.broadcasted_iota(jnp.int32, (TILE, size), 1)
    along = lambda x, l: jnp.broadcast_to(x[:, l : l + 1], (TILE, size))
    down = lambda x, j: jnp.broadcast_to(x[j : j + 1, :], (TILE, size))
    tiles = [block[row : row + TILE, :] for row in range(0, size, TILE)]
    outs = []
    for s, lines in enumerate(tiles):
        low = s * TILE
        inside = (lane >= low) & (lane < low + TILE)
        corner = [jnp.where(sub < TILE, along(lines, low + c), 0.0) for c in range(TILE)]
        lines = jnp.where(inside, jnp.where(lane - low == sub, 1.0, 0.0), lines)
        out = jnp.zeros((TILE, size), jnp.float32)
        same = jnp.ones((TILE, size), jnp.float32)
        cross = jnp.zeros((TILE, size), jnp.float32)
        for j in range(0, TILE, 2):
            both = (sub == j) | (sub == j + 1)
            left, right = corner[j], corner[j + 1]
            a, b, c = down(left, j), down(right, j), down(right, j + 1)
            inverse = 1.0 / (a * c - b * b)
            a_over, b_over, c_over = a * inverse, b * inverse, c * inverse
            first = jnp.where(both, 0.0, left * c_over - right * b_over)
            second = jnp.where(both, 0.0, right * a_over - left * b_over)
            upper, lower = down(lines, j), down(lines, j + 1)
            root = lax.rsqrt(a)
            ratio = b * (root * root)
            lower_out = (lower - ratio * upper) * lax.rsqrt(c - b * ratio)
            out = jnp.where(sub == j, upper * root, jnp.where(sub == j + 1, lower_out, out))
            same = jnp.where(sub == j, c_over, jnp.where(sub == j + 1, a_over, same))
            cross = jnp.where(both, b_over, cross)
            for k in range(j + 2, TILE):
                corner[k] = corner[k] - (first * down(corner[k], j) + second * down(corner[k], j + 1))
            lines = lines - (first * upper + second * lower)
        outs.append(jnp.where(lane < low + TILE, out, 0.0))
        partner = jnp.where(sub % 2 == 0, pltpu.roll(lines, TILE - 1, 0), pltpu.roll(lines, 1, 0))
        lines = lines * same - cross * partner
        rows = [down(lines, c) for c in range(TILE)]
        for t in range(s + 1, len(tiles)):
            terms = [along(tiles[t], low + c) * rows[c] for c in range(TILE)]
            while len(terms) > 1:
                terms = [x + y for x, y in zip(terms[::2], terms[1::2])]
            tiles[t] = jnp.where(inside, 0.0, tiles[t]) - terms[0]
    return jnp.concatenate(outs, axis=0)


def factor_kernel(gram_ref, far_ref, out_ref, work):
    size = gram_ref.shape[0]
    work[...] = gram_ref[...] + far_ref[...]
    for start in range(0, size, BLOCK):
        stop = start + BLOCK
        corner = inverse_factor(work[start:stop, start:stop])
        lane = lax.broadcasted_iota(jnp.int32, (BLOCK, size), 1)
        wide = jnp.concatenate(
            [jnp.zeros((BLOCK, start), jnp.float32)] * (start > 0)
            + [corner]
            + [jnp.zeros((BLOCK, size - stop), jnp.float32)] * (stop < size),
            axis=1,
        )
        lines = small_dot(corner, work[start:stop, :], ((1,), (0,)))
        lines = jnp.where((lane >= start) & (lane < stop), wide, lines)
        out_ref[start:stop, :] = jnp.where(lane < stop, lines, 0.0)
        if stop < size:
            factor = small_dot(work[stop:, start:stop], corner, ((1,), (1,)))
            lane = lax.broadcasted_iota(jnp.int32, (size - stop, size), 1)
            old = jnp.where((lane >= start) & (lane < stop), 0.0, work[stop:, :])
            work[stop:, :] = old - small_dot(factor, lines, ((1,), (0,)))


def inverse_cholesky(gram, far):
    whole = pl.BlockSpec(memory_space=pltpu.VMEM)
    return pl.pallas_call(
        factor_kernel,
        out_shape=jax.ShapeDtypeStruct(gram.shape, jnp.float32),
        in_specs=[whole, whole],
        out_specs=whole,
        scratch_shapes=[pltpu.VMEM(gram.shape, jnp.float32)],
        compiler_params=pltpu.CompilerParams(vmem_limit_bytes=16 << 20),
        cost_estimate=LIGHT,
    )(gram, far)


def after(values, *earlier):
    out = lax.optimization_barrier(tuple(values) + earlier)
    return out[: len(values)]


def exchanged(texture, sketch):
    col, row = lax.axis_index("cols"), lax.axis_index("rows")
    bits = lax.rem(col, 2), lax.rem(lax.div(col, 2), 2)

    def pairs(first_core, second_core):
        return [(8 * r + c, 8 * r + (c ^ step)) for r, step in ((0, first_core), (1, second_core)) for c in range(8)]

    line = pairs(4, 4)
    outer = [pairs(1, 2 if crossed else 1) for crossed in CROSSED]
    inner = [pairs(2, 1 if crossed else 2) for crossed in CROSSED]
    side = [jnp.where(row == 0, bits[0], bits[1]) if crossed else bits[0] for crossed in CROSSED]
    odd = [jnp.where(row == 0, bits[1], bits[0]) if crossed else bits[1] for crossed in CROSSED]
    chunks = range(len(SIZES))
    starts = [4 * sum(SIZES[:k]) for k in chunks]
    last = [None]

    def send(x, targets):
        last[0] = x
        return lax.ppermute(x, ("rows", "cols"), targets)

    def rows_of(k, which):
        return lax.dynamic_slice_in_dim(texture, starts[k] + which * (2 * SIZES[k]), 2 * SIZES[k])

    def part(x, which):
        return lax.dynamic_slice_in_dim(x, which * (x.shape[0] // 2), x.shape[0] // 2)

    def joined(k, own, other):
        return jnp.where(odd[k] == 0, jnp.concatenate([own, other]), jnp.concatenate([other, own]))

    arriving, own = {}, {}

    def placed(k, theirs, image):
        last[0] = image
        if theirs:
            arriving[k] = lax.ppermute(image, ("rows", "cols"), outer[k])
        else:
            own[k] = image

    def first_matmul(k, theirs):
        pinned = [pltpu.with_memory_space_constraint(x, pltpu.HBM) for x in (texture, sketch)]
        which = 1 - side[k] if theirs else side[k]
        parts = [(starts[k] + which * (2 * SIZES[k]), 2 * SIZES[k])]
        placed(k, theirs, sketched(*pinned, parts, [])[0])

    def matmul(k, theirs):
        (weights,) = after([sketch], last[0])
        rows = rows_of(k, 1 - side[k] if theirs else side[k])
        placed(k, theirs, jnp.dot(rows, weights, precision=HIGH, preferred_element_type=jnp.float32))

    kept, half, sums = {}, {}, [()]
    left = [name for name, *_ in STEPS if name in ("g", "f")]

    def arrived(k):
        return after([arriving[k]], last[0])[0]

    def to_inner(k):
        total = own[k] + arrived(k)
        kept[k] = part(total, odd[k])
        arriving[k] = send(part(total, 1 - odd[k]), inner[k])

    def to_line(k):
        kept[k] = kept[k] + arrived(k)
        arriving[k] = send(kept[k], line)

    def back_to_inner(k):
        kept[k] = kept[k] + arrived(k)
        arriving[k] = send(kept[k], inner[k])

    def back_to_outer(k):
        half[k] = joined(k, kept[k], arrived(k))
        arriving[k] = send(half[k], outer[k])

    def gather(rows, image):
        terms = inner_rows(image, image), inner_rows(image, rows)
        terms = tuple(map(jnp.add, sums[0], terms)) if sums[0] else terms
        left.pop()
        sums[0] = lax.optimization_barrier(terms) if left else terms
        last[0] = sums[0][0]

    def gather_own(k):
        gather(rows_of(k, side[k]), *after([half[k]], last[0]))

    def wait_far(k):
        arriving[k] = last[0] = arrived(k)

    def gather_far(k):
        gather(rows_of(k, 1 - side[k]), arrived(k))

    steps = dict(i=to_inner, l=to_line, b=back_to_inner, o=back_to_outer, g=gather_own, f=gather_far, w=wait_far, s=first_matmul, m=matmul)
    for name, *chunk in STEPS:
        steps[name](*chunk)
    return sums[0]


def per_device(texture, sketch):
    if lax.axis_size("cols") == 8 and texture.shape[0] == 4 * sum(SIZES):
        gram, product = exchanged(texture, sketch)
    else:
        partial = jnp.dot(texture, sketch, precision=HIGH, preferred_element_type=jnp.float32)
        image = lax.psum(partial, "cols")
        gram, product = inner_rows(image, image), inner_rows(image, texture)
    pair = [(0, 1), (1, 0)]
    far = lax.ppermute(gram, "rows", pair)
    inverse = inverse_cholesky(gram, far)
    (product,) = after([product], far)
    product = product + lax.ppermute(product, "rows", pair)
    span = gram.shape[0] // lax.axis_size("rows")
    inverse = lax.dynamic_slice_in_dim(inverse, lax.axis_index("rows") * span, span)
    return jnp.dot(inverse, product, precision=HIGH, preferred_element_type=jnp.float32)


def solution(mesh):
    placed = (P(("groups", "rows"), "cols"), P("cols", None))
    return jax.shard_map(
        per_device,
        mesh=mesh,
        in_specs=placed,
        out_specs=P(("groups", "rows"), "cols"),
        check_vma=False,
    )
```

```python
import functools

import jax
import jax.numpy as jnp
from jax import lax
from jax.experimental import pallas as pl
from jax.experimental.pallas import tpu as pltpu
from jax.sharding import PartitionSpec as P

HIGH = lax.Precision.HIGH
STEP = 256
SIZES = (128, 256, 128)
CROSSED = (True, True, True)
STEPS = [("s", 0, True), ("m", 1, True), ("m", 0, False), ("i", 0), ("m", 2, True), ("m", 1, False), ("l", 0), ("i", 1)]
STEPS += [("m", 2, False), ("i", 2), ("b", 0), ("l", 1), ("l", 2), ("b", 1), ("o", 0), ("w", 0), ("g", 0), ("o", 1), ("b", 2), ("f", 0), ("o", 2)]
STEPS += [("g", 1), ("f", 1), ("g", 2), ("f", 2)]
BLOCK = 128
TILE = 8
LIGHT = pl.CostEstimate(flops=1000, bytes_accessed=1000, transcendentals=0)


def split(x):
    high = x.astype(jnp.bfloat16)
    return high, (x - high.astype(jnp.float32)).astype(jnp.bfloat16)


def three_passes(left, right):
    (left_high, left_low), (right_high, right_low) = left, right
    dot = lambda x, y: jnp.dot(x, y, preferred_element_type=jnp.float32)
    return dot(left_high, right_high) + (dot(left_low, right_high) + dot(left_high, right_low))


def sketch_kernel(starts_ref, texture_ref, sketch_ref, *rest):
    outs, (blocks, sketch, sems) = rest[:-3], rest[-3:]
    count = blocks.shape[0]
    fetch = [pltpu.make_async_copy(sketch_ref, sketch, sems.at[count])]
    for k in range(count):
        start = pl.multiple_of(starts_ref[k], STEP)
        fetch.append(pltpu.make_async_copy(texture_ref.at[pl.ds(start, STEP), :], blocks.at[k], sems.at[k]))
    for copy in fetch:
        copy.start()
    fetch[0].wait()
    weights = split(sketch[...])
    k = 0
    for out in outs:
        for row in range(0, out.shape[0], STEP):
            fetch[k + 1].wait()
            out[row : row + STEP, :] = three_passes(split(blocks[k]), weights)
            k += 1


def sketched(texture, sketch, parts, earlier):
    starts = [first + row for first, length in parts for row in range(0, length, STEP)]
    (starts,) = after([jnp.stack(starts).astype(jnp.int32)], *earlier)
    count, (scans, rank) = starts.shape[0], sketch.shape
    there = pl.BlockSpec(memory_space=pl.ANY)
    return pl.pallas_call(
        sketch_kernel,
        out_shape=[jax.ShapeDtypeStruct((length, rank), jnp.float32) for _, length in parts],
        in_specs=[pl.BlockSpec(memory_space=pltpu.SMEM), there, there],
        out_specs=[pl.BlockSpec(memory_space=pltpu.VMEM)] * len(parts),
        scratch_shapes=[
            pltpu.VMEM((count, STEP, scans), jnp.float32),
            pltpu.VMEM((scans, rank), jnp.float32),
            pltpu.SemaphoreType.DMA((count + 1,)),
        ],
        compiler_params=pltpu.CompilerParams(vmem_limit_bytes=16 << 20),
        cost_estimate=pl.CostEstimate(
            flops=6 * count * STEP * scans * rank, bytes_accessed=4 * scans * (count * STEP + rank), transcendentals=0
        ),
    )(starts, texture, sketch)


def inner_rows(left, right):
    return lax.dot_general(
        left,
        right,
        (((0,), (0,)), ((), ())),
        precision=HIGH,
        preferred_element_type=jnp.float32,
    )


def small_dot(left, right, dims):
    return lax.dot_general(
        left,
        right,
        (dims, ((), ())),
        precision=lax.Precision.HIGHEST,
        preferred_element_type=jnp.float32,
    )


def inverse_factor(block):
    size = block.shape[0]
    sub = lax.broadcasted_iota(jnp.int32, (TILE, size), 0)
    lane = lax.broadcasted_iota(jnp.int32, (TILE, size), 1)
    along = lambda x, l: jnp.broadcast_to(x[:, l : l + 1], (TILE, size))
    down = lambda x, j: jnp.broadcast_to(x[j : j + 1, :], (TILE, size))
    tiles = [block[row : row + TILE, :] for row in range(0, size, TILE)]
    outs = []
    for s, lines in enumerate(tiles):
        low = s * TILE
        inside = (lane >= low) & (lane < low + TILE)
        corner = [jnp.where(sub < TILE, along(lines, low + c), 0.0) for c in range(TILE)]
        lines = jnp.where(inside, jnp.where(lane - low == sub, 1.0, 0.0), lines)
        out = jnp.zeros((TILE, size), jnp.float32)
        same = jnp.ones((TILE, size), jnp.float32)
        cross = jnp.zeros((TILE, size), jnp.float32)
        for j in range(0, TILE, 2):
            both = (sub == j) | (sub == j + 1)
            left, right = corner[j], corner[j + 1]
            a, b, c = down(left, j), down(right, j), down(right, j + 1)
            inverse = 1.0 / (a * c - b * b)
            a_over, b_over, c_over = a * inverse, b * inverse, c * inverse
            first = jnp.where(both, 0.0, left * c_over - right * b_over)
            second = jnp.where(both, 0.0, right * a_over - left * b_over)
            upper, lower = down(lines, j), down(lines, j + 1)
            root = lax.rsqrt(a)
            ratio = b * (root * root)
            lower_out = (lower - ratio * upper) * lax.rsqrt(c - b * ratio)
            out = jnp.where(sub == j, upper * root, jnp.where(sub == j + 1, lower_out, out))
            same = jnp.where(sub == j, c_over, jnp.where(sub == j + 1, a_over, same))
            cross = jnp.where(both, b_over, cross)
            for k in range(j + 2, TILE):
                corner[k] = corner[k] - (first * down(corner[k], j) + second * down(corner[k], j + 1))
            lines = lines - (first * upper + second * lower)
        outs.append(jnp.where(lane < low + TILE, out, 0.0))
        partner = jnp.where(sub % 2 == 0, pltpu.roll(lines, TILE - 1, 0), pltpu.roll(lines, 1, 0))
        lines = lines * same - cross * partner
        rows = [down(lines, c) for c in range(TILE)]
        for t in range(s + 1, len(tiles)):
            terms = [along(tiles[t], low + c) * rows[c] for c in range(TILE)]
            while len(terms) > 1:
                terms = [x + y for x, y in zip(terms[::2], terms[1::2])]
            tiles[t] = jnp.where(inside, 0.0, tiles[t]) - terms[0]
    return jnp.concatenate(outs, axis=0)


def factor_kernel(gram_ref, far_ref, out_ref, work):
    size = gram_ref.shape[0]
    root = lax.rsqrt(gram_ref[0:1, 0:1] + far_ref[0:1, 0:1])
    work[...] = (gram_ref[...] + far_ref[...]) * root * root
    for start in range(0, size, BLOCK):
        stop = start + BLOCK
        corner = inverse_factor(work[start:stop, start:stop])
        lane = lax.broadcasted_iota(jnp.int32, (BLOCK, size), 1)
        wide = jnp.concatenate(
            [jnp.zeros((BLOCK, start), jnp.float32)] * (start > 0)
            + [corner]
            + [jnp.zeros((BLOCK, size - stop), jnp.float32)] * (stop < size),
            axis=1,
        )
        lines = small_dot(corner, work[start:stop, :], ((1,), (0,)))
        lines = jnp.where((lane >= start) & (lane < stop), wide, lines)
        out_ref[start:stop, :] = jnp.where(lane < stop, lines, 0.0) * root
        if stop < size:
            factor = small_dot(work[stop:, start:stop], corner, ((1,), (1,)))
            lane = lax.broadcasted_iota(jnp.int32, (size - stop, size), 1)
            old = jnp.where((lane >= start) & (lane < stop), 0.0, work[stop:, :])
            work[stop:, :] = old - small_dot(factor, lines, ((1,), (0,)))


def inverse_cholesky(gram, far):
    whole = pl.BlockSpec(memory_space=pltpu.VMEM)
    return pl.pallas_call(
        factor_kernel,
        out_shape=jax.ShapeDtypeStruct(gram.shape, jnp.float32),
        in_specs=[whole, whole],
        out_specs=whole,
        scratch_shapes=[pltpu.VMEM(gram.shape, jnp.float32)],
        compiler_params=pltpu.CompilerParams(vmem_limit_bytes=16 << 20),
        cost_estimate=LIGHT,
    )(gram, far)


def after(values, *earlier):
    out = lax.optimization_barrier(tuple(values) + earlier)
    return out[: len(values)]


def exchanged(texture, sketch):
    col, row = lax.axis_index("cols"), lax.axis_index("rows")
    bits = lax.rem(col, 2), lax.rem(lax.div(col, 2), 2)

    def pairs(first_core, second_core):
        return [(8 * r + c, 8 * r + (c ^ step)) for r, step in ((0, first_core), (1, second_core)) for c in range(8)]

    line = pairs(4, 4)
    outer = [pairs(1, 2 if crossed else 1) for crossed in CROSSED]
    inner = [pairs(2, 1 if crossed else 2) for crossed in CROSSED]
    side = [jnp.where(row == 0, bits[0], bits[1]) if crossed else bits[0] for crossed in CROSSED]
    odd = [jnp.where(row == 0, bits[1], bits[0]) if crossed else bits[1] for crossed in CROSSED]
    chunks = range(len(SIZES))
    starts = [4 * sum(SIZES[:k]) for k in chunks]
    last = [None]

    def send(x, targets):
        last[0] = x
        return lax.ppermute(x, ("rows", "cols"), targets)

    def rows_of(k, which):
        return lax.dynamic_slice_in_dim(texture, starts[k] + which * (2 * SIZES[k]), 2 * SIZES[k])

    def part(x, which):
        return lax.dynamic_slice_in_dim(x, which * (x.shape[0] // 2), x.shape[0] // 2)

    def joined(k, own, other):
        return jnp.where(odd[k] == 0, jnp.concatenate([own, other]), jnp.concatenate([other, own]))

    arriving, own = {}, {}

    def placed(k, theirs, image):
        last[0] = image
        if theirs:
            arriving[k] = lax.ppermute(image, ("rows", "cols"), outer[k])
        else:
            own[k] = image

    def first_matmul(k, theirs):
        pinned = [pltpu.with_memory_space_constraint(x, pltpu.HBM) for x in (texture, sketch)]
        which = 1 - side[k] if theirs else side[k]
        parts = [(starts[k] + which * (2 * SIZES[k]), 2 * SIZES[k])]
        placed(k, theirs, sketched(*pinned, parts, [])[0])

    def matmul(k, theirs):
        (weights,) = after([sketch], last[0])
        rows = rows_of(k, 1 - side[k] if theirs else side[k])
        placed(k, theirs, jnp.dot(rows, weights, precision=HIGH, preferred_element_type=jnp.float32))

    kept, half, sums = {}, {}, [()]
    left = [name for name, *_ in STEPS if name in ("g", "f")]

    def arrived(k):
        return after([arriving[k]], last[0])[0]

    def to_inner(k):
        total = own[k] + arrived(k)
        kept[k] = part(total, odd[k])
        arriving[k] = send(part(total, 1 - odd[k]), inner[k])

    def to_line(k):
        kept[k] = kept[k] + arrived(k)
        arriving[k] = send(kept[k], line)

    def back_to_inner(k):
        kept[k] = kept[k] + arrived(k)
        arriving[k] = send(kept[k], inner[k])

    def back_to_outer(k):
        half[k] = joined(k, kept[k], arrived(k))
        arriving[k] = send(half[k], outer[k])

    def gather(rows, image):
        terms = inner_rows(image, image), inner_rows(image, rows)
        terms = tuple(map(jnp.add, sums[0], terms)) if sums[0] else terms
        left.pop()
        sums[0] = lax.optimization_barrier(terms) if left else terms
        last[0] = sums[0][0]

    def gather_own(k):
        gather(rows_of(k, side[k]), *after([half[k]], last[0]))

    def wait_far(k):
        arriving[k] = last[0] = arrived(k)

    def gather_far(k):
        gather(rows_of(k, 1 - side[k]), arrived(k))

    steps = dict(i=to_inner, l=to_line, b=back_to_inner, o=back_to_outer, g=gather_own, f=gather_far, w=wait_far, s=first_matmul, m=matmul)
    for name, *chunk in STEPS:
        steps[name](*chunk)
    return sums[0]


def per_device(texture, sketch):
    if lax.axis_size("cols") == 8 and texture.shape[0] == 4 * sum(SIZES):
        gram, product = exchanged(texture, sketch)
    else:
        partial = jnp.dot(texture, sketch, precision=HIGH, preferred_element_type=jnp.float32)
        image = lax.psum(partial, "cols")
        gram, product = inner_rows(image, image), inner_rows(image, texture)
    pair = [(0, 1), (1, 0)]
    far = lax.ppermute(gram, "rows", pair)
    inverse = inverse_cholesky(gram, far)
    (product,) = after([product], far)
    product = product + lax.ppermute(product, "rows", pair)
    span = gram.shape[0] // lax.axis_size("rows")
    inverse = lax.dynamic_slice_in_dim(inverse, lax.axis_index("rows") * span, span)
    return jnp.dot(inverse, product, precision=HIGH, preferred_element_type=jnp.float32)


def solution(mesh):
    placed = (P(("groups", "rows"), "cols"), P("cols", None))
    return jax.shard_map(
        per_device,
        mesh=mesh,
        in_specs=placed,
        out_specs=P(("groups", "rows"), "cols"),
        check_vma=False,
    )
```

```python
import functools

import jax
import jax.numpy as jnp
from jax import lax
from jax.experimental import pallas as pl
from jax.experimental.pallas import tpu as pltpu
from jax.sharding import PartitionSpec as P

HIGH = lax.Precision.HIGH
STEP = 256
SIZES = (128, 256, 128)
CROSSED = (True, True, True)
STEPS = [("s", 0, True), ("m", 1, True), ("m", 0, False), ("i", 0), ("m", 2, True), ("m", 1, False), ("l", 0), ("i", 1)]
STEPS += [("m", 2, False), ("i", 2), ("b", 0), ("l", 1), ("l", 2), ("b", 1), ("o", 0), ("w", 0), ("g", 0), ("o", 1), ("b", 2), ("f", 0), ("o", 2)]
STEPS += [("g", 1), ("f", 1), ("g", 2), ("f", 2)]
BLOCK = 128
TILE = 8
LIGHT = pl.CostEstimate(flops=1000, bytes_accessed=1000, transcendentals=0)


def split(x):
    high = x.astype(jnp.bfloat16)
    return high, (x - high.astype(jnp.float32)).astype(jnp.bfloat16)


def three_passes(left, right):
    (left_high, left_low), (right_high, right_low) = left, right
    dot = lambda x, y: jnp.dot(x, y, preferred_element_type=jnp.float32)
    return dot(left_high, right_high) + (dot(left_low, right_high) + dot(left_high, right_low))


def sketch_kernel(starts_ref, texture_ref, sketch_ref, *rest):
    outs, (blocks, sketch, sems) = rest[:-3], rest[-3:]
    count = blocks.shape[0]
    fetch = [pltpu.make_async_copy(sketch_ref, sketch, sems.at[count])]
    for k in range(count):
        start = pl.multiple_of(starts_ref[k], STEP)
        fetch.append(pltpu.make_async_copy(texture_ref.at[pl.ds(start, STEP), :], blocks.at[k], sems.at[k]))
    for copy in fetch:
        copy.start()
    fetch[0].wait()
    weights = split(sketch[...])
    k = 0
    for out in outs:
        for row in range(0, out.shape[0], STEP):
            fetch[k + 1].wait()
            out[row : row + STEP, :] = three_passes(split(blocks[k]), weights)
            k += 1


def sketched(texture, sketch, parts, earlier):
    starts = [first + row for first, length in parts for row in range(0, length, STEP)]
    (starts,) = after([jnp.stack(starts).astype(jnp.int32)], *earlier)
    count, (scans, rank) = starts.shape[0], sketch.shape
    there = pl.BlockSpec(memory_space=pl.ANY)
    return pl.pallas_call(
        sketch_kernel,
        out_shape=[jax.ShapeDtypeStruct((length, rank), jnp.float32) for _, length in parts],
        in_specs=[pl.BlockSpec(memory_space=pltpu.SMEM), there, there],
        out_specs=[pl.BlockSpec(memory_space=pltpu.VMEM)] * len(parts),
        scratch_shapes=[
            pltpu.VMEM((count, STEP, scans), jnp.float32),
            pltpu.VMEM((scans, rank), jnp.float32),
            pltpu.SemaphoreType.DMA((count + 1,)),
        ],
        compiler_params=pltpu.CompilerParams(vmem_limit_bytes=16 << 20),
        cost_estimate=pl.CostEstimate(
            flops=6 * count * STEP * scans * rank, bytes_accessed=4 * scans * (count * STEP + rank), transcendentals=0
        ),
    )(starts, texture, sketch)


def inner_rows(left, right):
    return lax.dot_general(
        left,
        right,
        (((0,), (0,)), ((), ())),
        precision=HIGH,
        preferred_element_type=jnp.float32,
    )


def small_dot(left, right, dims):
    return lax.dot_general(
        left,
        right,
        (dims, ((), ())),
        precision=lax.Precision.HIGHEST,
        preferred_element_type=jnp.float32,
    )


def inverse_factor(block):
    size = block.shape[0]
    sub = lax.broadcasted_iota(jnp.int32, (TILE, size), 0)
    lane = lax.broadcasted_iota(jnp.int32, (TILE, size), 1)
    along = lambda x, l: jnp.broadcast_to(x[:, l : l + 1], (TILE, size))
    down = lambda x, j: jnp.broadcast_to(x[j : j + 1, :], (TILE, size))
    tiles = [block[row : row + TILE, :] for row in range(0, size, TILE)]
    outs = []
    for s, lines in enumerate(tiles):
        low = s * TILE
        inside = (lane >= low) & (lane < low + TILE)
        corner = [jnp.where(sub < TILE, along(lines, low + c), 0.0) for c in range(TILE)]
        lines = jnp.where(inside, jnp.where(lane - low == sub, 1.0, 0.0), lines)
        out = jnp.zeros((TILE, size), jnp.float32)
        same = jnp.ones((TILE, size), jnp.float32)
        cross = jnp.zeros((TILE, size), jnp.float32)
        for j in range(0, TILE, 2):
            both = (sub == j) | (sub == j + 1)
            left, right = corner[j], corner[j + 1]
            a, b, c = down(left, j), down(right, j), down(right, j + 1)
            inverse = 1.0 / (a * c - b * b)
            a_over, b_over, c_over = a * inverse, b * inverse, c * inverse
            first = jnp.where(both, 0.0, left * c_over - right * b_over)
            second = jnp.where(both, 0.0, right * a_over - left * b_over)
            upper, lower = down(lines, j), down(lines, j + 1)
            root = lax.rsqrt(a)
            ratio = b * (root * root)
            lower_out = (lower - ratio * upper) * lax.rsqrt(c - b * ratio)
            out = jnp.where(sub == j, upper * root, jnp.where(sub == j + 1, lower_out, out))
            same = jnp.where(sub == j, c_over, jnp.where(sub == j + 1, a_over, same))
            cross = jnp.where(both, b_over, cross)
            for k in range(j + 2, TILE):
                corner[k] = corner[k] - (first * down(corner[k], j) + second * down(corner[k], j + 1))
            lines = lines - (first * upper + second * lower)
        outs.append(jnp.where(lane < low + TILE, out, 0.0))
        partner = jnp.where(sub % 2 == 0, pltpu.roll(lines, TILE - 1, 0), pltpu.roll(lines, 1, 0))
        lines = lines * same - cross * partner
        rows = [down(lines, c) for c in range(TILE)]
        for t in range(s + 1, len(tiles)):
            terms = [along(tiles[t], low + c) * rows[c] for c in range(TILE)]
            while len(terms) > 1:
                terms = [x + y for x, y in zip(terms[::2], terms[1::2])]
            tiles[t] = jnp.where(inside, 0.0, tiles[t]) - terms[0]
    return jnp.concatenate(outs, axis=0)


def factor_kernel(gram_ref, far_ref, out_ref, work):
    size = gram_ref.shape[0]
    root = lax.rsqrt(gram_ref[0:1, 0:1] + far_ref[0:1, 0:1])
    work[...] = (gram_ref[...] + far_ref[...]) * root * root
    for start in range(0, size, BLOCK):
        stop = start + BLOCK
        corner = inverse_factor(work[start:stop, start:stop])
        rest = stop < size
        if rest:
            right = small_dot(corner, work[start:stop, stop:], ((1,), (0,)))
            factor = small_dot(work[stop:, start:stop], corner, ((1,), (1,)))
            work[stop:, stop:] = work[stop:, stop:] - small_dot(factor, right, ((1,), (0,)))
            work[stop:, start:stop] = -small_dot(factor, corner, ((1,), (0,)))
            out_ref[start:stop, stop:] = jnp.zeros((BLOCK, size - stop), jnp.float32)
        out_ref[start:stop, start:stop] = corner * root
        if start > 0:
            left = small_dot(corner, work[start:stop, :start], ((1,), (0,)))
            out_ref[start:stop, :start] = left * root
            if rest:
                work[stop:, :start] = work[stop:, :start] - small_dot(factor, left, ((1,), (0,)))


def inverse_cholesky(gram, far):
    whole = pl.BlockSpec(memory_space=pltpu.VMEM)
    return pl.pallas_call(
        factor_kernel,
        out_shape=jax.ShapeDtypeStruct(gram.shape, jnp.float32),
        in_specs=[whole, whole],
        out_specs=whole,
        scratch_shapes=[pltpu.VMEM(gram.shape, jnp.float32)],
        compiler_params=pltpu.CompilerParams(vmem_limit_bytes=16 << 20),
        cost_estimate=LIGHT,
    )(gram, far)


def after(values, *earlier):
    out = lax.optimization_barrier(tuple(values) + earlier)
    return out[: len(values)]


def exchanged(texture, sketch):
    col, row = lax.axis_index("cols"), lax.axis_index("rows")
    bits = lax.rem(col, 2), lax.rem(lax.div(col, 2), 2)

    def pairs(first_core, second_core):
        return [(8 * r + c, 8 * r + (c ^ step)) for r, step in ((0, first_core), (1, second_core)) for c in range(8)]

    line = pairs(4, 4)
    outer = [pairs(1, 2 if crossed else 1) for crossed in CROSSED]
    inner = [pairs(2, 1 if crossed else 2) for crossed in CROSSED]
    side = [jnp.where(row == 0, bits[0], bits[1]) if crossed else bits[0] for crossed in CROSSED]
    odd = [jnp.where(row == 0, bits[1], bits[0]) if crossed else bits[1] for crossed in CROSSED]
    chunks = range(len(SIZES))
    starts = [4 * sum(SIZES[:k]) for k in chunks]
    last = [None]

    def send(x, targets):
        last[0] = x
        return lax.ppermute(x, ("rows", "cols"), targets)

    def rows_of(k, which):
        return lax.dynamic_slice_in_dim(texture, starts[k] + which * (2 * SIZES[k]), 2 * SIZES[k])

    def part(x, which):
        return lax.dynamic_slice_in_dim(x, which * (x.shape[0] // 2), x.shape[0] // 2)

    def joined(k, own, other):
        return jnp.where(odd[k] == 0, jnp.concatenate([own, other]), jnp.concatenate([other, own]))

    arriving, own = {}, {}

    def placed(k, theirs, image):
        last[0] = image
        if theirs:
            arriving[k] = lax.ppermute(image, ("rows", "cols"), outer[k])
        else:
            own[k] = image

    def first_matmul(k, theirs):
        pinned = [pltpu.with_memory_space_constraint(x, pltpu.HBM) for x in (texture, sketch)]
        which = 1 - side[k] if theirs else side[k]
        parts = [(starts[k] + which * (2 * SIZES[k]), 2 * SIZES[k])]
        placed(k, theirs, sketched(*pinned, parts, [])[0])

    def matmul(k, theirs):
        (weights,) = after([sketch], last[0])
        rows = rows_of(k, 1 - side[k] if theirs else side[k])
        placed(k, theirs, jnp.dot(rows, weights, precision=HIGH, preferred_element_type=jnp.float32))

    kept, half, sums = {}, {}, [()]
    left = [name for name, *_ in STEPS if name in ("g", "f")]

    def arrived(k):
        return after([arriving[k]], last[0])[0]

    def to_inner(k):
        total = own[k] + arrived(k)
        kept[k] = part(total, odd[k])
        arriving[k] = send(part(total, 1 - odd[k]), inner[k])

    def to_line(k):
        kept[k] = kept[k] + arrived(k)
        arriving[k] = send(kept[k], line)

    def back_to_inner(k):
        kept[k] = kept[k] + arrived(k)
        arriving[k] = send(kept[k], inner[k])

    def back_to_outer(k):
        half[k] = joined(k, kept[k], arrived(k))
        arriving[k] = send(half[k], outer[k])

    def gather(rows, image):
        terms = inner_rows(image, image), inner_rows(image, rows)
        terms = tuple(map(jnp.add, sums[0], terms)) if sums[0] else terms
        left.pop()
        sums[0] = lax.optimization_barrier(terms) if left else terms
        last[0] = sums[0][0]

    def gather_own(k):
        gather(rows_of(k, side[k]), *after([half[k]], last[0]))

    def wait_far(k):
        arriving[k] = last[0] = arrived(k)

    def gather_far(k):
        gather(rows_of(k, 1 - side[k]), arrived(k))

    steps = dict(i=to_inner, l=to_line, b=back_to_inner, o=back_to_outer, g=gather_own, f=gather_far, w=wait_far, s=first_matmul, m=matmul)
    for name, *chunk in STEPS:
        steps[name](*chunk)
    return sums[0]


def per_device(texture, sketch):
    if lax.axis_size("cols") == 8 and texture.shape[0] == 4 * sum(SIZES):
        gram, product = exchanged(texture, sketch)
    else:
        partial = jnp.dot(texture, sketch, precision=HIGH, preferred_element_type=jnp.float32)
        image = lax.psum(partial, "cols")
        gram, product = inner_rows(image, image), inner_rows(image, texture)
    pair = [(0, 1), (1, 0)]
    far = lax.ppermute(gram, "rows", pair)
    inverse = inverse_cholesky(gram, far)
    (product,) = after([product], far)
    product = product + lax.ppermute(product, "rows", pair)
    span = gram.shape[0] // lax.axis_size("rows")
    inverse = lax.dynamic_slice_in_dim(inverse, lax.axis_index("rows") * span, span)
    return jnp.dot(inverse, product, precision=HIGH, preferred_element_type=jnp.float32)


def solution(mesh):
    placed = (P(("groups", "rows"), "cols"), P("cols", None))
    return jax.shard_map(
        per_device,
        mesh=mesh,
        in_specs=placed,
        out_specs=P(("groups", "rows"), "cols"),
        check_vma=False,
    )
```

```python
import functools

import jax
import jax.numpy as jnp
from jax import lax
from jax.experimental import pallas as pl
from jax.experimental.pallas import tpu as pltpu
from jax.sharding import PartitionSpec as P

HIGH = lax.Precision.HIGH
STEP = 256
SIZES = (128, 256, 128)
CROSSED = (True, True, True)
STEPS = [("s", 0, True), ("m", 1, True), ("m", 0, False), ("i", 0), ("m", 2, True), ("m", 1, False), ("l", 0), ("i", 1)]
STEPS += [("m", 2, False), ("i", 2), ("b", 0), ("l", 1), ("l", 2), ("b", 1), ("o", 0), ("w", 0), ("g", 0), ("o", 1), ("b", 2), ("f", 0), ("o", 2)]
STEPS += [("g", 1), ("g", 2), ("f", 1), ("f", 2)]
BLOCK = 128
TILE = 8
LIGHT = pl.CostEstimate(flops=1000, bytes_accessed=1000, transcendentals=0)


def split(x):
    high = x.astype(jnp.bfloat16)
    return high, (x - high.astype(jnp.float32)).astype(jnp.bfloat16)


def three_passes(left, right):
    (left_high, left_low), (right_high, right_low) = left, right
    dot = lambda x, y: jnp.dot(x, y, preferred_element_type=jnp.float32)
    return dot(left_high, right_high) + (dot(left_low, right_high) + dot(left_high, right_low))


def sketch_kernel(starts_ref, texture_ref, sketch_ref, *rest):
    outs, (blocks, sketch, sems) = rest[:-3], rest[-3:]
    count = blocks.shape[0]
    fetch = [pltpu.make_async_copy(sketch_ref, sketch, sems.at[count])]
    for k in range(count):
        start = pl.multiple_of(starts_ref[k], STEP)
        fetch.append(pltpu.make_async_copy(texture_ref.at[pl.ds(start, STEP), :], blocks.at[k], sems.at[k]))
    for copy in fetch:
        copy.start()
    fetch[0].wait()
    weights = split(sketch[...])
    k = 0
    for out in outs:
        for row in range(0, out.shape[0], STEP):
            fetch[k + 1].wait()
            out[row : row + STEP, :] = three_passes(split(blocks[k]), weights)
            k += 1


def sketched(texture, sketch, parts, earlier):
    starts = [first + row for first, length in parts for row in range(0, length, STEP)]
    (starts,) = after([jnp.stack(starts).astype(jnp.int32)], *earlier)
    count, (scans, rank) = starts.shape[0], sketch.shape
    there = pl.BlockSpec(memory_space=pl.ANY)
    return pl.pallas_call(
        sketch_kernel,
        out_shape=[jax.ShapeDtypeStruct((length, rank), jnp.float32) for _, length in parts],
        in_specs=[pl.BlockSpec(memory_space=pltpu.SMEM), there, there],
        out_specs=[pl.BlockSpec(memory_space=pltpu.VMEM)] * len(parts),
        scratch_shapes=[
            pltpu.VMEM((count, STEP, scans), jnp.float32),
            pltpu.VMEM((scans, rank), jnp.float32),
            pltpu.SemaphoreType.DMA((count + 1,)),
        ],
        compiler_params=pltpu.CompilerParams(vmem_limit_bytes=16 << 20),
        cost_estimate=pl.CostEstimate(
            flops=6 * count * STEP * scans * rank, bytes_accessed=4 * scans * (count * STEP + rank), transcendentals=0
        ),
    )(starts, texture, sketch)


def inner_rows(left, right):
    return lax.dot_general(
        left,
        right,
        (((0,), (0,)), ((), ())),
        precision=HIGH,
        preferred_element_type=jnp.float32,
    )


def small_dot(left, right, dims):
    return lax.dot_general(
        left,
        right,
        (dims, ((), ())),
        precision=lax.Precision.HIGHEST,
        preferred_element_type=jnp.float32,
    )


def inverse_factor(block):
    size = block.shape[0]
    sub = lax.broadcasted_iota(jnp.int32, (TILE, size), 0)
    lane = lax.broadcasted_iota(jnp.int32, (TILE, size), 1)
    along = lambda x, l: jnp.broadcast_to(x[:, l : l + 1], (TILE, size))
    down = lambda x, j: jnp.broadcast_to(x[j : j + 1, :], (TILE, size))
    tiles = [block[row : row + TILE, :] for row in range(0, size, TILE)]
    outs = []
    for s, lines in enumerate(tiles):
        low = s * TILE
        inside = (lane >= low) & (lane < low + TILE)
        corner = [jnp.where(sub < TILE, along(lines, low + c), 0.0) for c in range(TILE)]
        lines = jnp.where(inside, jnp.where(lane - low == sub, 1.0, 0.0), lines)
        out = jnp.zeros((TILE, size), jnp.float32)
        same = jnp.ones((TILE, size), jnp.float32)
        cross = jnp.zeros((TILE, size), jnp.float32)
        for j in range(0, TILE, 2):
            both = (sub == j) | (sub == j + 1)
            left, right = corner[j], corner[j + 1]
            a, b, c = down(left, j), down(right, j), down(right, j + 1)
            inverse = 1.0 / (a * c - b * b)
            a_over, b_over, c_over = a * inverse, b * inverse, c * inverse
            first = jnp.where(both, 0.0, left * c_over - right * b_over)
            second = jnp.where(both, 0.0, right * a_over - left * b_over)
            upper, lower = down(lines, j), down(lines, j + 1)
            root = lax.rsqrt(a)
            ratio = b * (root * root)
            lower_out = (lower - ratio * upper) * lax.rsqrt(c - b * ratio)
            out = jnp.where(sub == j, upper * root, jnp.where(sub == j + 1, lower_out, out))
            same = jnp.where(sub == j, c_over, jnp.where(sub == j + 1, a_over, same))
            cross = jnp.where(both, b_over, cross)
            for k in range(j + 2, TILE):
                corner[k] = corner[k] - (first * down(corner[k], j) + second * down(corner[k], j + 1))
            lines = lines - (first * upper + second * lower)
        outs.append(jnp.where(lane < low + TILE, out, 0.0))
        partner = jnp.where(sub % 2 == 0, pltpu.roll(lines, TILE - 1, 0), pltpu.roll(lines, 1, 0))
        lines = lines * same - cross * partner
        rows = [down(lines, c) for c in range(TILE)]
        for t in range(s + 1, len(tiles)):
            terms = [along(tiles[t], low + c) * rows[c] for c in range(TILE)]
            while len(terms) > 1:
                terms = [x + y for x, y in zip(terms[::2], terms[1::2])]
            tiles[t] = jnp.where(inside, 0.0, tiles[t]) - terms[0]
    return jnp.concatenate(outs, axis=0)


def factor_kernel(gram_ref, far_ref, out_ref, work):
    size = gram_ref.shape[0]
    root = lax.rsqrt(gram_ref[0:1, 0:1] + far_ref[0:1, 0:1])
    work[...] = (gram_ref[...] + far_ref[...]) * root * root
    for start in range(0, size, BLOCK):
        stop = start + BLOCK
        corner = inverse_factor(work[start:stop, start:stop])
        rest = stop < size
        if rest:
            right = small_dot(corner, work[start:stop, stop:], ((1,), (0,)))
            factor = small_dot(work[stop:, start:stop], corner, ((1,), (1,)))
            work[stop:, stop:] = work[stop:, stop:] - small_dot(factor, right, ((1,), (0,)))
            work[stop:, start:stop] = -small_dot(factor, corner, ((1,), (0,)))
            out_ref[start:stop, stop:] = jnp.zeros((BLOCK, size - stop), jnp.float32)
        out_ref[start:stop, start:stop] = corner * root
        if start > 0:
            left = small_dot(corner, work[start:stop, :start], ((1,), (0,)))
            out_ref[start:stop, :start] = left * root
            if rest:
                work[stop:, :start] = work[stop:, :start] - small_dot(factor, left, ((1,), (0,)))


def inverse_cholesky(gram, far):
    whole = pl.BlockSpec(memory_space=pltpu.VMEM)
    return pl.pallas_call(
        factor_kernel,
        out_shape=jax.ShapeDtypeStruct(gram.shape, jnp.float32),
        in_specs=[whole, whole],
        out_specs=whole,
        scratch_shapes=[pltpu.VMEM(gram.shape, jnp.float32)],
        compiler_params=pltpu.CompilerParams(vmem_limit_bytes=16 << 20),
        cost_estimate=LIGHT,
    )(gram, far)


def after(values, *earlier):
    out = lax.optimization_barrier(tuple(values) + earlier)
    return out[: len(values)]


def exchanged(texture, sketch):
    col, row = lax.axis_index("cols"), lax.axis_index("rows")
    bits = lax.rem(col, 2), lax.rem(lax.div(col, 2), 2)

    def pairs(first_core, second_core):
        return [(8 * r + c, 8 * r + (c ^ step)) for r, step in ((0, first_core), (1, second_core)) for c in range(8)]

    line = pairs(4, 4)
    outer = [pairs(1, 2 if crossed else 1) for crossed in CROSSED]
    inner = [pairs(2, 1 if crossed else 2) for crossed in CROSSED]
    side = [jnp.where(row == 0, bits[0], bits[1]) if crossed else bits[0] for crossed in CROSSED]
    odd = [jnp.where(row == 0, bits[1], bits[0]) if crossed else bits[1] for crossed in CROSSED]
    chunks = range(len(SIZES))
    starts = [4 * sum(SIZES[:k]) for k in chunks]
    last = [None]

    def send(x, targets):
        last[0] = x
        return lax.ppermute(x, ("rows", "cols"), targets)

    def rows_of(k, which):
        return lax.dynamic_slice_in_dim(texture, starts[k] + which * (2 * SIZES[k]), 2 * SIZES[k])

    def part(x, which):
        return lax.dynamic_slice_in_dim(x, which * (x.shape[0] // 2), x.shape[0] // 2)

    def joined(k, own, other):
        return jnp.where(odd[k] == 0, jnp.concatenate([own, other]), jnp.concatenate([other, own]))

    arriving, own = {}, {}

    def placed(k, theirs, image):
        last[0] = image
        if theirs:
            arriving[k] = lax.ppermute(image, ("rows", "cols"), outer[k])
        else:
            own[k] = image

    def first_matmul(k, theirs):
        pinned = [pltpu.with_memory_space_constraint(x, pltpu.HBM) for x in (texture, sketch)]
        which = 1 - side[k] if theirs else side[k]
        parts = [(starts[k] + which * (2 * SIZES[k]), 2 * SIZES[k])]
        placed(k, theirs, sketched(*pinned, parts, [])[0])

    def matmul(k, theirs):
        (weights,) = after([sketch], last[0])
        rows = rows_of(k, 1 - side[k] if theirs else side[k])
        placed(k, theirs, jnp.dot(rows, weights, precision=HIGH, preferred_element_type=jnp.float32))

    kept, half, sums = {}, {}, [()]
    left = [name for name, *_ in STEPS if name in ("g", "f")]

    def arrived(k):
        return after([arriving[k]], last[0])[0]

    def to_inner(k):
        total = own[k] + arrived(k)
        kept[k] = part(total, odd[k])
        arriving[k] = send(part(total, 1 - odd[k]), inner[k])

    def to_line(k):
        kept[k] = kept[k] + arrived(k)
        arriving[k] = send(kept[k], line)

    def back_to_inner(k):
        kept[k] = kept[k] + arrived(k)
        arriving[k] = send(kept[k], inner[k])

    def back_to_outer(k):
        half[k] = joined(k, kept[k], arrived(k))
        arriving[k] = send(half[k], outer[k])

    def gather(rows, image):
        terms = inner_rows(image, image), inner_rows(image, rows)
        terms = tuple(map(jnp.add, sums[0], terms)) if sums[0] else terms
        left.pop()
        sums[0] = lax.optimization_barrier(terms) if left else terms
        last[0] = sums[0][0]

    def gather_own(k):
        gather(rows_of(k, side[k]), *after([half[k]], last[0]))

    def wait_far(k):
        arriving[k] = last[0] = arrived(k)

    def gather_far(k):
        gather(rows_of(k, 1 - side[k]), arrived(k))

    steps = dict(i=to_inner, l=to_line, b=back_to_inner, o=back_to_outer, g=gather_own, f=gather_far, w=wait_far, s=first_matmul, m=matmul)
    for name, *chunk in STEPS:
        steps[name](*chunk)
    return sums[0]


def per_device(texture, sketch):
    if lax.axis_size("cols") == 8 and texture.shape[0] == 4 * sum(SIZES):
        gram, product = exchanged(texture, sketch)
    else:
        partial = jnp.dot(texture, sketch, precision=HIGH, preferred_element_type=jnp.float32)
        image = lax.psum(partial, "cols")
        gram, product = inner_rows(image, image), inner_rows(image, texture)
    pair = [(0, 1), (1, 0)]
    far = lax.ppermute(gram, "rows", pair)
    inverse = inverse_cholesky(gram, far)
    (product,) = after([product], far)
    product = product + lax.ppermute(product, "rows", pair)
    span = gram.shape[0] // lax.axis_size("rows")
    inverse = lax.dynamic_slice_in_dim(inverse, lax.axis_index("rows") * span, span)
    return jnp.dot(inverse, product, precision=HIGH, preferred_element_type=jnp.float32)


def solution(mesh):
    placed = (P(("groups", "rows"), "cols"), P("cols", None))
    return jax.shard_map(
        per_device,
        mesh=mesh,
        in_specs=placed,
        out_specs=P(("groups", "rows"), "cols"),
        check_vma=False,
    )
```
